32 devices in a mesh: dp: 4 (over y, core), row: 2 (over x), col: 4 (over z).
Axes of the slice: x: 2, y: 2, z: 4, core: 2. Of those that a mesh axis runs over, the one named last changes fastest.
Arguments:
- tokens: bfloat16 [8192, 1024], P(('dp', 'row'), 'col'), may hold values from -6 to 6
- passages: bfloat16 [32, 300, 1024], P(('dp', 'row'), None, 'col'), may hold values from -6 to 6
- lengths: int32 [8], replicated, may hold values from 256 to 1792, as said below
- block_order: int32 [64], replicated, may hold values from 0 to 63, as said below
- passage_ids: int32 [8, 5], replicated, may hold values from 0 to 31, as said below
- triple_weight: bfloat16 [1024, 3, 1024], P('col', None, 'row'), may hold values from -0.1875 to 0.1875
- self_out_weight: bfloat16 [1024, 1024], P('row', 'col'), may hold values from -2 to 2
- query_weight: bfloat16 [1024, 1, 1024], P('col', None, 'row'), may hold values from -0.1875 to 0.1875
- memory_weight: bfloat16 [1024, 2, 1024], P('col', None, 'row'), may hold values from -0.1875 to 0.1875
- cross_out_weight: bfloat16 [1024, 1024], P('row', 'col'), may hold values from -4 to 4
- expand_weight: bfloat16 [1024, 1, 4096], P('col', None, 'row'), may hold values from -0.1875 to 0.1875
- contract_weight: bfloat16 [4096, 1024], P('row', 'col'), may hold values from -0.09375 to 0.09375
- norm_gain: bfloat16 [3, 1024], P(None, 'col'), may hold values from 0.25 to 1.75
- norm_bias: bfloat16 [3, 1024], P(None, 'col'), may hold values from -1.5 to 1.5
- cotangent: bfloat16 [8192, 1024], P(('dp', 'row'), 'col'), may hold values from -6 to 6
Outputs:
- output: bfloat16 [8192, 1024], P(('dp', 'row'), 'col')
- grad_tokens: bfloat16 [8192, 1024], P(('dp', 'row'), 'col')
- grad_passages: bfloat16 [32, 300, 1024], P(('dp', 'row'), None, 'col')
- grad_triple: float32 [1024, 3, 1024], P('col', None, 'row')
- grad_self_out: float32 [1024, 1024], P('row', 'col')
- grad_query: float32 [1024, 1, 1024], P('col', None, 'row')
- grad_memory: float32 [1024, 2, 1024], P('col', None, 'row')
- grad_cross_out: float32 [1024, 1024], P('row', 'col')
- grad_expand: float32 [1024, 1, 4096], P('col', None, 'row')
- grad_contract: float32 [4096, 1024], P('row', 'col')
- grad_norm_gain: float32 [3, 1024], P(None, 'col')
- grad_norm_bias: float32 [3, 1024], P(None, 'col')
The draws below stay inside these ranges and needn't reach their ends.
Inputs may be any that keep to these rules, and one draw needn't show every extreme that they name: For every group g the lengths 2g and 2g + 1 sum to 2048; some group holds a sequence of exactly 256 tokens. `block_order`: A permutation of the blocks that keeps every block at its index of row: the block of group order q = (g * 2 + r) * 8 + j comes from a given-order block with the same r. The blocks of one index of dp and row in given order go to exactly 2 groups, 4 to each, and the blocks of one index of dp and row in group order come from exactly 2 groups, 4 from each. `passage_ids`: each sequence names 5 different passages of its own group's pool (g * 8 to (g + 1) * 8 - 1 for group g), and each passage of a pool is named by one of the group's two sequences.
All inputs are finite; a program needn't handle non-finite values.
Results may differ from the reference program's by a relative error of at most 0.03.
Values may be sent and summed in bfloat16 or wider, within the bound.
No kernel may reach another device: no remote copies, remote signals or barrier semaphores. Data moves between devices by JAX's collectives and lax.ppermute only.
A program may use at most 192 MiB of HBM per device.

```python
import jax
import jax.numpy as jnp
from jax import lax

D = 1024
HEADS = 16
HD = 64
FF = 4096
PLEN = 300
TOPP = 5
PP_GRP = 8
MINLEN = 256
BLK = 128
TOK_ROW = 1024
TOK_GRP = 2048
TOKENS = 8192
SEQS = 8
PASSAGES = 32


def draw_lengths(key, part):
    groups = SEQS // 2
    leeway = TOK_GRP - 2 * MINLEN
    firsts = MINLEN + jax.random.randint(jax.random.fold_in(key, 1), (groups,), 0, leeway + 1, dtype=jnp.int32)
    forced = jax.random.randint(jax.random.fold_in(key, 2), (), 0, groups, dtype=jnp.int32)
    firsts = jnp.where(jnp.arange(groups, dtype=jnp.int32) == forced, MINLEN, firsts)
    return jnp.stack([firsts, TOK_GRP - firsts], 1).reshape(-1).astype(jnp.int32)


def shuffled_blocks(subkey, count):
    return jax.random.permutation(subkey, count)


def draw_block_order(key, part):
    groups = TOKENS // TOK_GRP
    rows_per = TOK_GRP // TOK_ROW
    blocks = TOK_ROW // BLK
    fanout = groups // 2
    capacity = blocks // fanout
    order = jnp.zeros((TOKENS // BLK,), jnp.int32)
    for row_index in range(rows_per):
        subkey = jax.random.fold_in(key, 10 + row_index)
        keys = jax.random.split(subkey, 4)
        shifts = jax.random.permutation(keys[0], groups)[:fanout]
        row_perm = jax.random.permutation(keys[1], groups)
        col_perm = jax.random.permutation(keys[2], groups)
        slot_keys = jax.random.split(keys[3], groups + 1)
        source_slots = jax.vmap(partial_blocks(blocks))(slot_keys[:groups])
        link = jnp.arange(blocks, dtype=jnp.int32) // capacity
        target_group = col_perm[(row_perm[:, None] + shifts[link][None, :]) % groups]
        ranking = jax.random.permutation(slot_keys[groups], groups * blocks)
        flat_target = target_group.reshape(-1)
        position = jnp.sum((flat_target[None, :] == flat_target[:, None]) & (ranking[None, :] < ranking[:, None]), 1)
        target = (flat_target * rows_per + row_index) * blocks + position
        source = ((jnp.arange(groups, dtype=jnp.int32)[:, None] * rows_per + row_index) * blocks + source_slots).reshape(-1)
        order = order.at[target.astype(jnp.int32)].set(source.astype(jnp.int32))
    return order.astype(jnp.int32)


def partial_blocks(count):

    def shuffle(subkey):
        return shuffled_blocks(subkey, count)
    return shuffle


def draw_passage_ids(key, part):
    groups = PASSAGES // PP_GRP

    def one_group(index):
        subkey = jax.random.fold_in(key, index)
        keys = jax.random.split(subkey, 2)
        first_order = jax.random.permutation(keys[0], PP_GRP)
        reuse = jax.random.permutation(keys[1], TOPP)[:2 * TOPP - PP_GRP]
        second = jnp.concatenate([first_order[TOPP:], first_order[reuse]])
        return jnp.stack([first_order[:TOPP], second]) + index * PP_GRP
    return jax.vmap(one_group)(jnp.arange(groups, dtype=jnp.int32)).reshape(-1, TOPP).astype(jnp.int32)


def steps_of(rng, shape, shards, least, high):
    factor_of = 1.0
    for dim, blocks in shards:
        draws = jax.random.uniform(jax.random.fold_in(jax.random.fold_in(rng, 6), dim), (blocks,), jnp.float32, least / len(shards), high / len(shards))
        factor_of = factor_of * jnp.repeat(jnp.exp(draws), shape[dim] // blocks).reshape((-1,) + (1,) * (len(shape) - 1 - dim))
    return factor_of


def bell_draw(rng, extent, scale, most, cuts=(), kind=jnp.bfloat16):
    values = scale * jax.random.normal(rng, extent, jnp.float32)
    if cuts:
        values = values * steps_of(rng, extent, cuts, -0.22, 0.18)
    return jnp.clip(values, -most, most).astype(kind)


def setup_inputs(seed: int = 0) -> dict:
    key_list = jax.random.split(jax.random.key(seed), 16)
    return {
        "tokens": bell_draw(key_list[0], (TOKENS, D), 1.0, 6.0, ((0, 8), (1, 4))),
        "passages": bell_draw(key_list[1], (PASSAGES, PLEN, D), 1.0, 6.0, ((0, 8), (2, 4))),
        "lengths": draw_lengths(jax.random.fold_in(key_list[15], 71), 0),
        "block_order": draw_block_order(jax.random.fold_in(key_list[15], 71), 0),
        "passage_ids": draw_passage_ids(jax.random.fold_in(key_list[15], 71), 0),
        "triple_weight": bell_draw(key_list[5], (D, 3, D), D ** -0.5, 0.1875, ((0, 4), (2, 2))),
        "self_out_weight": bell_draw(key_list[6], (D, D), (max(1, D // (MINLEN // 2))) ** -0.5, 2.0, ((0, 2), (1, 4))),
        "query_weight": bell_draw(key_list[7], (D, 1, D), D ** -0.5, 0.1875, ((0, 4), (2, 2))),
        "memory_weight": bell_draw(key_list[8], (D, 2, D), D ** -0.5, 0.1875, ((0, 4), (2, 2))),
        "cross_out_weight": bell_draw(key_list[9], (D, D), (max(1, D // (TOPP * PLEN // 4))) ** -0.5, 4.0, ((0, 2), (1, 4))),
        "expand_weight": bell_draw(key_list[10], (D, 1, FF), D ** -0.5, 0.1875, ((0, 4), (2, 2))),
        "contract_weight": bell_draw(key_list[11], (FF, D), FF ** -0.5, 0.09375, ((0, 2), (1, 4))),
        "norm_gain": jnp.clip(1.0 + 0.15 * jax.random.normal(key_list[12], (3, D), jnp.float32), 0.25, 1.75).astype(jnp.bfloat16),
        "norm_bias": bell_draw(key_list[13], (3, D), 0.3, 1.5, ((1, 4),)),
        "cotangent": bell_draw(key_list[14], (TOKENS, D), 1.0, 6.0, ((0, 8), (1, 4))),
    }


highest = lax.Precision.HIGHEST
epsilon = 1e-05
masked_out = -1000000000.0

@jax.custom_vjp
def low(v):
    return lax.optimization_barrier(v.astype(jnp.bfloat16)).astype(jnp.float32)

@jax.custom_vjp
def low_back(v):
    return v

def low_keep(v):
    return (low(v), None)

def low_pass(kept, grad):
    return (grad,)

def back_keep(v):
    return (v, None)

def back_low(kept, grad):
    return (low(grad),)
low.defvjp(low_keep, low_pass)
low_back.defvjp(back_keep, back_low)

def matmul(left, right):
    return jnp.dot(left, right, precision=highest, preferred_element_type=jnp.float32)

def project(rows, weight):
    return jnp.einsum('rf,fke->rke', rows, weight, precision=highest, preferred_element_type=jnp.float32)

def layer_norm(value, gain, offset):
    center = value - lax.optimization_barrier(jnp.mean(value, -1, keepdims=True))
    spread = lax.optimization_barrier(jnp.mean(center * center, -1, keepdims=True))
    return center * lax.rsqrt(spread + epsilon) * gain + offset

def self_mask(first, total):

    def allowed(start, count):
        query_pos = start + jnp.arange(count, dtype=jnp.int32)
        key_pos = jnp.arange(total, dtype=jnp.int32)
        begin = jnp.where(query_pos >= first, first, 0)
        return (key_pos[None, :] <= query_pos[:, None]) & (key_pos[None, :] >= begin[:, None])
    return allowed

def cross_mask(first, chosen_ids, key_count):
    key_passage = jnp.arange(key_count, dtype=jnp.int32) // PLEN
    member = jnp.any(key_passage[None, None, :] == chosen_ids[:, :, None], 1)

    def allowed(start, count):
        query_pos = start + jnp.arange(count, dtype=jnp.int32)
        later = (query_pos >= first)[:, None]
        return jnp.where(later, member[1][None, :], member[0][None, :])
    return allowed

def attention(queries, keys, values, allowed):
    total = queries.shape[0]
    block = min(512, total)
    factor = HD ** (-0.5)

    def one_block(index):
        start = index * block
        chosen = lax.dynamic_slice_in_dim(queries, start, block, 0)
        scores = jnp.einsum('qhe,khe->hqk', chosen, keys, precision=highest, preferred_element_type=jnp.float32) * factor
        scores = low_back(scores)
        scores = jnp.where(allowed(start, block)[None], scores, masked_out)
        top = lax.optimization_barrier(jnp.max(scores, -1, keepdims=True))
        expo = jnp.exp(scores - top)
        probs = low(expo / lax.optimization_barrier(jnp.sum(expo, -1, keepdims=True)))
        return jnp.einsum('hqk,khe->qhe', probs, values, precision=highest, preferred_element_type=jnp.float32)
    blocks = lax.map(jax.checkpoint(one_block), jnp.arange(total // block, dtype=jnp.int32))
    return blocks.reshape(total, -1)

def layer(inputs, memory, triple_weight, self_out_weight, query_weight, memory_weight, cross_out_weight, expand_weight, contract_weight, norm_gain, norm_bias, first, chosen_ids):
    total = inputs.shape[0]
    triple = low_back(low(project(inputs, triple_weight))).reshape(total, 3, HEADS, HD)
    attended = low_back(low(attention(triple[:, 0], triple[:, 1], triple[:, 2], self_mask(first, total))))
    first_sum = inputs + low_back(matmul(attended, self_out_weight))
    normed_one = layer_norm(first_sum, norm_gain[0], norm_bias[0])
    queries = low_back(low(project(low(normed_one), query_weight))).reshape(total, HEADS, HD)
    pairs = low_back(low(project(memory, memory_weight))).reshape(-1, 2, HEADS, HD)
    crossed = low_back(low(attention(queries, pairs[:, 0], pairs[:, 1], cross_mask(first, chosen_ids, memory.shape[0]))))
    second_sum = normed_one + low_back(matmul(crossed, cross_out_weight))
    normed_two = layer_norm(second_sum, norm_gain[1], norm_bias[1])
    hidden = low_back(project(low(normed_two), expand_weight)[:, 0])
    active = low(jax.nn.gelu(hidden, approximate=False))
    third_sum = normed_two + low_back(matmul(active, contract_weight))
    return layer_norm(third_sum, norm_gain[2], norm_bias[2])

def reference(tokens, passages, lengths, block_order, passage_ids, triple_weight, self_out_weight, query_weight, memory_weight, cross_out_weight, expand_weight, contract_weight, norm_gain, norm_bias, cotangent):
    groups = TOKENS // TOK_GRP
    offsets = jnp.arange(BLK, dtype=jnp.int32)
    given_rows = (block_order[:, None] * BLK + offsets[None, :]).reshape(-1).astype(jnp.int32)
    inputs = tokens.astype(jnp.float32)[given_rows].reshape(groups, TOK_GRP, D)
    upstream = cotangent.astype(jnp.float32)[given_rows].reshape(groups, TOK_GRP, D)
    memory = passages.astype(jnp.float32).reshape(groups, PP_GRP * PLEN, D)
    firsts = lengths.reshape(groups, 2)[:, 0]
    local_ids = passage_ids.reshape(groups, 2, TOPP) - (jnp.arange(groups, dtype=jnp.int32) * PP_GRP)[:, None, None]
    params = tuple((weight.astype(jnp.float32) for weight in (triple_weight, self_out_weight, query_weight, memory_weight, cross_out_weight, expand_weight, contract_weight, norm_gain, norm_bias)))

    def per_group(totals, item):
        group_in, group_memory, group_up, first, chosen_ids = item

        def run_layer(value, memory_rows, *weights):
            return layer(value, memory_rows, *weights, first, chosen_ids)
        result, pullback = jax.vjp(run_layer, group_in, group_memory, *params)
        grads = pullback(group_up)
        totals = tuple((running + fresh for running, fresh in zip(totals, grads[2:])))
        return (totals, (result, grads[0], grads[1]))
    start = tuple((jnp.zeros(param.shape, jnp.float32) for param in params))
    totals, (results, grad_inputs, grad_memory) = lax.scan(per_group, start, (inputs, memory, upstream, firsts, local_ids))
    output = jnp.zeros((TOKENS, D), jnp.float32).at[given_rows].set(results.reshape(-1, D)).astype(jnp.bfloat16)
    grad_tokens = jnp.zeros((TOKENS, D), jnp.float32).at[given_rows].set(grad_inputs.reshape(-1, D)).astype(jnp.bfloat16)
    grad_passages = grad_memory.reshape(PASSAGES, PLEN, D).astype(jnp.bfloat16)
    return (output, grad_tokens, grad_passages, totals[0], totals[1], totals[2], totals[3], totals[4], totals[5], totals[6], totals[7], totals[8])
```

```python
import jax
import jax.numpy as jnp
from jax import lax
from jax.experimental import pallas as pl
from jax.experimental.pallas import tpu as pltpu
from jax.sharding import PartitionSpec as P

HD = 64
PAIR = 2 * HD
PLEN = 300
TOPP = 5
PP_GRP = 8
BLK = 128
SPAN = 304


epsilon = 1e-05
LOW = -1e30
FACTOR = HD ** (-0.5)


def swap_row(value):
    return lax.ppermute(value, "row", [(0, 1), (1, 0)])


def to_tokens(rows):
    cols = lax.axis_size("col")
    count, width = rows.shape
    got = lax.all_to_all(rows.reshape(cols, count // cols, width), "col", 0, 0, tiled=True)
    return got.transpose(1, 0, 2).reshape(count // cols, cols * width)


def to_features(rows):
    cols = lax.axis_size("col")
    count, width = rows.shape
    parts = rows.reshape(count, cols, width // cols).transpose(1, 0, 2)
    return lax.all_to_all(parts, "col", 0, 0, tiled=True).reshape(count * cols, width // cols)


def to_heads(rows):
    return to_features(rows)


def from_heads(rows):
    return to_tokens(rows)


def regroup(value, select, placing, groups):
    width = value.shape[-1]
    out = value.reshape(-1, BLK, width)[select]
    moved = lax.all_to_all(out, "dp", split_axis=0, concat_axis=0, tiled=True)
    return moved[placing].reshape(-1, width)


def gather_in(weight):
    return lax.all_gather(weight, "col", axis=0, tiled=True)


def gather_out(weight):
    return lax.all_gather(weight, "col", axis=0, tiled=False)


def dot(left, right):
    return jnp.dot(left, right, preferred_element_type=jnp.float32)


def in_proj(rows, weight):
    return jnp.einsum("tf,fe->te", rows, weight, preferred_element_type=jnp.float32)


def in_proj_back(grad, weight):
    return jnp.einsum("te,fe->tf", grad, weight, preferred_element_type=jnp.float32)


def out_proj(rows, weight):
    out = jnp.einsum("te,cef->tcf", rows, weight, preferred_element_type=jnp.float32)
    return out.reshape(rows.shape[0], -1)


def out_proj_back(grad, weight):
    parts = grad.reshape(grad.shape[0], weight.shape[0], weight.shape[2])
    return jnp.einsum("tcf,cef->te", parts, weight, preferred_element_type=jnp.float32)


def in_weight_grad(rows, grad):
    return jnp.einsum("tf,te->fe", rows, grad, preferred_element_type=jnp.float32).astype(
        jnp.bfloat16
    )


def out_weight_grad(rows, grad, cols):
    parts = grad.reshape(grad.shape[0], cols, -1)
    return jnp.einsum("te,tcf->cef", rows, parts, preferred_element_type=jnp.float32).astype(
        jnp.bfloat16
    )


def reduce_weight(grad):
    cols = lax.axis_size("col")
    flat = grad.reshape(-1, grad.shape[-1])
    part = lax.psum_scatter(flat, ("col", "dp"), scatter_dimension=0, tiled=True)
    return lax.all_gather(part, "dp", axis=0, tiled=True).astype(jnp.float32)


def both_halves(part):
    own = part.shape[0] // 2
    low = part.astype(jnp.bfloat16)
    upper = part[:own] + swap_row(low[own:]).astype(jnp.float32)
    lower = part[own:] + swap_row(low[:own]).astype(jnp.float32)
    return jnp.concatenate([upper, lower], 0)


def norm_forward(value, gain, offset):
    center = jnp.mean(value, 1, keepdims=True)
    moved = value - center
    scale = lax.rsqrt(jnp.mean(moved * moved, 1, keepdims=True) + epsilon)
    normed = moved * scale
    return (normed * gain + offset, normed, scale)


def norm_back(grad, normed, scale, gain):
    scaled = grad * gain
    total = jnp.mean(scaled, 1, keepdims=True)
    crossed = jnp.mean(scaled * normed, 1, keepdims=True)
    return scale * (scaled - total - normed * crossed)


def norm_param_sums(grad, normed, own):
    return (jnp.sum(grad[:own] * normed[:own], 0), jnp.sum(grad[:own], 0))


def nt(left, right):
    return lax.dot_general(
        left, right, (((1,), (1,)), ((), ())), preferred_element_type=jnp.float32
    )


def nn(left, right):
    return jnp.dot(left, right, preferred_element_type=jnp.float32)


def flip(value):
    return value.astype(jnp.float32).T.astype(jnp.bfloat16)


def stack_heads(value):
    lane = lax.broadcasted_iota(jnp.int32, value.shape, 1) // HD
    wide = value.astype(jnp.float32)
    parts = [jnp.where(lane == h, wide, 0.0) for h in range(2)]
    return jnp.concatenate(parts, 0).astype(jnp.bfloat16)


def fresh_state(count):
    return (
        jnp.full((1, count), LOW, jnp.float32),
        jnp.zeros((1, count), jnp.float32),
        jnp.zeros((HD, count), jnp.float32),
    )


def per_head(flipped, wide):
    count = wide.shape[1] // 2
    return jnp.concatenate(
        [nn(flipped[h * HD : (h + 1) * HD], wide[:, h * count : (h + 1) * count]) for h in range(2)],
        1,
    )


def step_forward(state, scores, v_flipped):
    top, total, out = state
    fresh = jnp.maximum(top, jnp.max(scores, 0, keepdims=True))
    keep = jnp.exp(top - fresh)
    expo = jnp.exp(scores - fresh)
    total = total * keep + jnp.sum(expo, 0, keepdims=True)
    out = out * keep + per_head(v_flipped, expo.astype(jnp.bfloat16))
    return (fresh, total, out)


def rows_of(out):
    count = out.shape[1] // 2
    return jnp.concatenate([out[:, :count], out[:, count:]], 0).T


def finish_forward(state, o_ref, lse_ref):
    top, total, out = state
    o_ref[...] = rows_of(out / total).astype(jnp.bfloat16)
    lse_ref[...] = (top + jnp.log(total)).reshape(lse_ref.shape)


def delta_of(out, up):
    both = (out.astype(jnp.float32) * up.astype(jnp.float32)).T
    return jnp.concatenate(
        [jnp.sum(both[h * HD : (h + 1) * HD], 0, keepdims=True) for h in range(2)], 1
    )


def step_backward(scores, lse, delta, value, up, queries, k_flipped):
    probs = jnp.exp(scores - lse)
    grad_value = nn(probs.astype(jnp.bfloat16), up)
    grad_scores = (probs * (nt(value, up) - delta)).astype(jnp.bfloat16)
    return grad_value, nn(grad_scores, queries), per_head(k_flipped, grad_scores)


def self_spans(i, first, tile):
    start = i * tile
    begin = jnp.where(start >= first, first, 0)
    begin_last = jnp.where(start + tile - 1 >= first, first, 0)
    low = begin // tile
    middle = jnp.minimum((begin_last + tile - 1) // tile, i)
    return low, jnp.maximum(middle, low)


def self_masked(scores, i, j, first, tile):
    count = scores.shape[1]
    key_pos = j * tile + lax.broadcasted_iota(jnp.int32, scores.shape, 0)
    lane = lax.broadcasted_iota(jnp.int32, (1, count), 1)
    query_pos = i * tile + jnp.where(lane >= tile, lane - tile, lane)
    begin = jnp.where(query_pos >= first, first, 0)
    return jnp.where((key_pos <= query_pos) & (key_pos >= begin), scores, LOW)


def self_forward_kernel(tiles, tile, info, q_ref, k_ref, v_ref, o_ref, lse_ref, v_flipped):
    i = pl.program_id(0)
    first = info[tiles]

    @pl.when(i == 0)
    def _():
        for j in range(tiles):
            v_flipped[j] = flip(v_ref[j * tile : (j + 1) * tile, :])

    queries = stack_heads(q_ref[...].astype(jnp.float32) * FACTOR)
    low, middle = self_spans(i, first, tile)

    def visit(masked):
        def body(j, state):
            at = info[j]
            keys = k_ref[pl.ds(pl.multiple_of(at * tile, tile), tile), :]
            scores = nt(keys, queries)
            if masked:
                scores = self_masked(scores, i, j, first, tile)
            return step_forward(state, scores, v_flipped[at])

        return body

    state = fresh_state(2 * tile)
    state = lax.fori_loop(low, middle, visit(True), state)
    state = lax.fori_loop(middle, i, visit(False), state)
    finish_forward(visit(True)(i, state), o_ref, lse_ref)


def self_backward_kernel(
    tiles, tile, info, q_ref, k_ref, v_ref, o_ref, up_ref, lse_ref,
    dq_ref, dk_ref, dv_ref, k_flipped, dk_sum, dv_sum,
):
    i = pl.program_id(0)
    first = info[tiles]

    @pl.when(i == 0)
    def _():
        for j in range(tiles):
            k_flipped[j] = flip(k_ref[j * tile : (j + 1) * tile, :])
        dk_sum[...] = jnp.zeros_like(dk_sum)
        dv_sum[...] = jnp.zeros_like(dv_sum)

    queries = stack_heads(q_ref[...].astype(jnp.float32) * FACTOR)
    up = stack_heads(up_ref[...])
    delta = delta_of(o_ref[...], up_ref[...])
    lse = lse_ref[...].reshape(1, 2 * tile)
    low, middle = self_spans(i, first, tile)

    def visit(masked):
        def body(j, total):
            at = info[j]
            rows = pl.ds(pl.multiple_of(at * tile, tile), tile)
            scores = nt(k_ref[rows, :], queries)
            if masked:
                scores = self_masked(scores, i, j, first, tile)
            gv, gk, gq = step_backward(
                scores, lse, delta, v_ref[rows, :], up, queries, k_flipped[at]
            )
            dv_sum[rows, :] += gv
            dk_sum[rows, :] += gk
            return total + gq

        return body

    total = jnp.zeros((HD, 2 * tile), jnp.float32)
    total = lax.fori_loop(low, middle, visit(True), total)
    total = lax.fori_loop(middle, i, visit(False), total)
    total = visit(True)(i, total)
    dq_ref[...] = (rows_of(total) * FACTOR).astype(jnp.bfloat16)

    @pl.when(i == tiles - 1)
    def _():
        dk_ref[...] = dk_sum[...].astype(jnp.bfloat16)
        dv_ref[...] = dv_sum[...].astype(jnp.bfloat16)


def cost(flops, elements, size):
    return pl.CostEstimate(flops=flops, bytes_accessed=size, transcendentals=elements)


def self_attend(q, k, v, info, tile):
    total = q.shape[0]
    tiles = total // tile
    part = pl.BlockSpec((tile, PAIR), lambda i, info: (info[i], 0))
    whole = pl.BlockSpec((total, PAIR), lambda i, info: (0, 0))
    stat = pl.BlockSpec((1, 1, 2 * tile), lambda i, info: (i, 0, 0))
    elements = total * total
    return pl.pallas_call(
        lambda *refs: self_forward_kernel(tiles, tile, *refs),
        out_shape=(
            jax.ShapeDtypeStruct((total, PAIR), jnp.bfloat16),
            jax.ShapeDtypeStruct((tiles, 1, 2 * tile), jnp.float32),
        ),
        grid_spec=pltpu.PrefetchScalarGridSpec(
            num_scalar_prefetch=1,
            grid=(tiles,),
            in_specs=[part, whole, whole],
            out_specs=(part, stat),
            scratch_shapes=[pltpu.VMEM((tiles, PAIR, tile), jnp.bfloat16)],
        ),
        cost_estimate=cost(8 * elements * PAIR, elements, 4 * total * PAIR * 2),
        name="self_attend",
    )(info, q, k, v)


def self_attend_back(q, k, v, out, up, lse, info, tile):
    total = q.shape[0]
    tiles = total // tile
    part = pl.BlockSpec((tile, PAIR), lambda i, info: (info[i], 0))
    whole = pl.BlockSpec((total, PAIR), lambda i, info: (0, 0))
    stat = pl.BlockSpec((1, 1, 2 * tile), lambda i, info: (i, 0, 0))
    elements = total * total
    like = jax.ShapeDtypeStruct((total, PAIR), jnp.bfloat16)
    return pl.pallas_call(
        lambda *refs: self_backward_kernel(tiles, tile, *refs),
        out_shape=(like, like, like),
        grid_spec=pltpu.PrefetchScalarGridSpec(
            num_scalar_prefetch=1,
            grid=(tiles,),
            in_specs=[part, whole, whole, part, part, stat],
            out_specs=(part, whole, whole),
            scratch_shapes=[
                pltpu.VMEM((tiles, PAIR, tile), jnp.bfloat16),
                pltpu.VMEM((total, PAIR), jnp.float32),
                pltpu.VMEM((total, PAIR), jnp.float32),
            ],
        ),
        cost_estimate=cost(20 * elements * PAIR, elements, 8 * total * PAIR * 2),
        name="self_attend_back",
    )(info, q, k, v, out, up, lse)


def cross_scores(keys, queries, bias, valid):
    scores = nt(keys, queries) + bias
    tail = scores.shape[0] - 8
    row = lax.broadcasted_iota(jnp.int32, (8, scores.shape[1]), 0)
    return jnp.concatenate(
        [scores[:tail], jnp.where(row < valid - tail, scores[tail:], LOW)], 0
    )


def cross_bias(info, side, passages, at, count):
    base = side * (passages + 2)
    switch = info[base + passages + 1]
    flags = info[2 * (passages + 2) + at]
    lane = lax.broadcasted_iota(jnp.int32, (1, 2 * count), 1)
    place = jnp.where(lane >= count, lane - count, lane)
    reads = jnp.where(place < switch, flags & 1, flags >> 1)
    return jnp.where(reads > 0, 0.0, LOW)


def cross_forward_kernel(passages, span, valid, info, q_ref, k_ref, v_ref, o_ref, lse_ref, v_flipped):
    side = pl.program_id(1)
    count = q_ref.shape[0]

    @pl.when(side == 0)
    def _():
        for j in range(passages):
            v_flipped[j] = flip(v_ref[j * span : (j + 1) * span, :])

    queries = stack_heads(q_ref[...].astype(jnp.float32) * FACTOR)
    base = side * (passages + 2)

    def body(t, state):
        at = info[base + t]
        keys = k_ref[pl.ds(pl.multiple_of(at * span, 16), span), :]
        scores = cross_scores(keys, queries, cross_bias(info, side, passages, at, count), valid)
        return step_forward(state, scores, v_flipped[at])

    state = lax.fori_loop(0, info[base + passages], body, fresh_state(2 * count))
    finish_forward(state, o_ref, lse_ref)


def cross_backward_kernel(
    passages, span, valid, info, q_ref, k_ref, v_ref, o_ref, up_ref, lse_ref,
    dq_ref, dkv_ref, k_flipped, dk_sum, dv_sum,
):
    pair = pl.program_id(0)
    side = pl.program_id(1)
    count = q_ref.shape[0]

    @pl.when(side == 0)
    def _():
        for j in range(passages):
            k_flipped[j] = flip(k_ref[j * span : (j + 1) * span, :])
        dk_sum[...] = jnp.zeros_like(dk_sum)
        dv_sum[...] = jnp.zeros_like(dv_sum)

    queries = stack_heads(q_ref[...].astype(jnp.float32) * FACTOR)
    up = stack_heads(up_ref[...])
    delta = delta_of(o_ref[...], up_ref[...])
    lse = lse_ref[...].reshape(1, 2 * count)
    base = side * (passages + 2)

    def body(t, total):
        at = info[base + t]
        rows = pl.ds(pl.multiple_of(at * span, 16), span)
        scores = cross_scores(
            k_ref[rows, :], queries, cross_bias(info, side, passages, at, count), valid
        )
        gv, gk, gq = step_backward(scores, lse, delta, v_ref[rows, :], up, queries, k_flipped[at])
        dv_sum[rows, :] += gv
        dk_sum[rows, :] += gk
        return total + gq

    total = jnp.zeros((HD, 2 * count), jnp.float32)
    total = lax.fori_loop(0, info[base + passages], body, total)
    dq_ref[...] = (rows_of(total) * FACTOR).astype(jnp.bfloat16)

    @pl.when(side == 1)
    def _():
        pairs = pl.num_programs(0)
        width = dkv_ref.shape[1] // 2
        dkv_ref[:, pl.ds(pl.multiple_of(pair * PAIR, PAIR), PAIR)] = dk_sum[...].astype(jnp.bfloat16)
        dkv_ref[:, pl.ds(pl.multiple_of(width + pair * PAIR, PAIR), PAIR)] = dv_sum[...].astype(
            jnp.bfloat16
        )


def cross_attend(q, kv, info, passages, valid):
    rows, width = q.shape
    keys = kv.shape[0]
    pairs = width // PAIR
    count = rows // 2
    span = keys // passages
    part = pl.BlockSpec((count, PAIR), lambda p, s, info: (s, p))
    k_spec = pl.BlockSpec((keys, PAIR), lambda p, s, info: (0, p))
    v_spec = pl.BlockSpec((keys, PAIR), lambda p, s, info: (0, pairs + p))
    stat = pl.BlockSpec((1, 1, 1, 2 * count), lambda p, s, info: (p, s, 0, 0))
    elements = rows * keys * 2 * pairs
    return pl.pallas_call(
        lambda *refs: cross_forward_kernel(passages, span, valid, *refs),
        out_shape=(
            jax.ShapeDtypeStruct((rows, width), jnp.bfloat16),
            jax.ShapeDtypeStruct((pairs, 2, 1, 2 * count), jnp.float32),
        ),
        grid_spec=pltpu.PrefetchScalarGridSpec(
            num_scalar_prefetch=1,
            grid=(pairs, 2),
            in_specs=[part, k_spec, v_spec],
            out_specs=(part, stat),
            scratch_shapes=[pltpu.VMEM((passages, PAIR, span), jnp.bfloat16)],
        ),
        cost_estimate=cost(8 * elements * PAIR, elements, kv.size * 2),
        name="cross_attend",
    )(info, q, kv, kv)


def cross_attend_back(q, kv, out, up, lse, info, passages, valid):
    rows, width = q.shape
    keys = kv.shape[0]
    pairs = width // PAIR
    count = rows // 2
    span = keys // passages
    part = pl.BlockSpec((count, PAIR), lambda p, s, info: (s, p))
    k_spec = pl.BlockSpec((keys, PAIR), lambda p, s, info: (0, p))
    v_spec = pl.BlockSpec((keys, PAIR), lambda p, s, info: (0, pairs + p))
    whole = pl.BlockSpec((keys, 2 * width), lambda p, s, info: (0, 0))
    stat = pl.BlockSpec((1, 1, 1, 2 * count), lambda p, s, info: (p, s, 0, 0))
    elements = rows * keys * 2 * pairs
    return pl.pallas_call(
        lambda *refs: cross_backward_kernel(passages, span, valid, *refs),
        out_shape=(
            jax.ShapeDtypeStruct((rows, width), jnp.bfloat16),
            jax.ShapeDtypeStruct((keys, 2 * width), jnp.bfloat16),
        ),
        grid_spec=pltpu.PrefetchScalarGridSpec(
            num_scalar_prefetch=1,
            grid=(pairs, 2),
            in_specs=[part, k_spec, v_spec, part, part, stat],
            out_specs=(part, whole),
            scratch_shapes=[
                pltpu.VMEM((passages, PAIR, span), jnp.bfloat16),
                pltpu.VMEM((keys, PAIR), jnp.float32),
                pltpu.VMEM((keys, PAIR), jnp.float32),
            ],
        ),
        cost_estimate=cost(20 * elements * PAIR, elements, kv.size * 6),
        name="cross_attend_back",
    )(info, q, kv, kv, out, up, lse)


def gelu_exact(value):
    return jax.nn.gelu(value, approximate=False)


def on_device(
    tokens,
    passages,
    lengths,
    block_order,
    passage_ids,
    triple_weight,
    self_out_weight,
    query_weight,
    memory_weight,
    cross_out_weight,
    expand_weight,
    contract_weight,
    norm_gain,
    norm_bias,
    cotangent,
):
    groups = lax.axis_size("dp")
    row_count = lax.axis_size("row")
    cols = lax.axis_size("col")
    group = lax.axis_index("dp")
    row_index = lax.axis_index("row")
    col_index = lax.axis_index("col")
    own_rows, width = tokens.shape
    features = width * cols
    blocks = own_rows // BLK
    capacity = blocks // (groups // 2)
    span = row_count * blocks
    all_blocks = block_order.shape[0]
    block_ids = jnp.arange(blocks, dtype=jnp.int32)
    slot_ids = jnp.arange(groups * capacity, dtype=jnp.int32)
    inverse = (
        jnp.zeros_like(block_order).at[block_order].set(jnp.arange(all_blocks, dtype=jnp.int32))
    )
    own_blocks = (group * row_count + row_index) * blocks + block_ids
    target = inverse[own_blocks] // span
    earlier = block_ids[None, :] < block_ids[:, None]
    ranking = jnp.sum((target[None, :] == target[:, None]) & earlier, 1)
    matches = (target[None, :] == (slot_ids // capacity)[:, None]) & (
        ranking[None, :] == (slot_ids % capacity)[:, None]
    )
    send_select = jnp.sum(jnp.where(matches, block_ids[None, :], 0), 1)
    back_place = target * capacity + ranking
    wanted = block_order[own_blocks]
    source = wanted // span
    within = wanted % blocks
    rank_in = jnp.sum((source[None, :] == source[:, None]) & (within[None, :] < within[:, None]), 1)
    recv_place = source * capacity + rank_in
    back_matches = recv_place[None, :] == slot_ids[:, None]
    back_select = jnp.sum(jnp.where(back_matches, block_ids[None, :], 0), 1)

    total = own_rows * row_count
    own = own_rows // cols
    first = lax.dynamic_slice_in_dim(lengths, group * 2, 1)[0]
    chosen_ids = lax.dynamic_slice(passage_ids, (group * 2, 0), (2, TOPP)) - group * PP_GRP

    tile_ids = jnp.arange(row_count * cols, dtype=jnp.int32)
    self_info = jnp.concatenate(
        [(tile_ids % cols) * row_count + ((tile_ids // cols) ^ row_index), first[None]]
    )
    pool = passages.shape[0]
    held_passage = ((tile_ids % row_count) ^ row_index) * pool + tile_ids // row_count
    reads = jnp.any(held_passage[None, None, :] == chosen_ids[:, :, None], 1)
    side = jnp.arange(row_count, dtype=jnp.int32)
    switch = jnp.clip(first - (side ^ row_index) * own_rows - col_index * own, 0, own)
    needed = ((switch > 0)[:, None] & reads[0][None]) | ((switch < own)[:, None] & reads[1][None])
    needed = needed.astype(jnp.int32)
    before = jnp.sum(
        needed[:, None, :] * (tile_ids[None, None, :] < tile_ids[None, :, None]), 2
    )
    slots = needed[:, :, None] * (before[:, :, None] == tile_ids[None, None, :])
    listed = jnp.sum(slots * tile_ids[None, :, None], 1)
    per_side = jnp.concatenate([listed, jnp.sum(needed, 1)[:, None], switch[:, None]], 1)
    flags = reads[0].astype(jnp.int32) + 2 * reads[1].astype(jnp.int32)
    cross_info = jnp.concatenate([per_side.reshape(-1), flags]).astype(jnp.int32)
    passage_count = row_count * pool

    def take_tokens(value):
        mine = to_tokens(regroup(value, send_select, recv_place, groups))
        return jnp.concatenate([mine, swap_row(mine)], 0)

    rows_in = take_tokens(tokens)
    upstream = take_tokens(cotangent)
    memory_own = to_tokens(passages.reshape(-1, width))
    memory_own = jnp.pad(memory_own, ((0, SPAN - memory_own.shape[0]), (0, 0)))
    memory = jnp.concatenate([memory_own, swap_row(memory_own)], 0)

    triple_w = gather_in(triple_weight.reshape(width, -1))
    memory_w = gather_in(memory_weight.reshape(width, -1))
    self_out_w = gather_out(self_out_weight)
    query_w = gather_in(query_weight.reshape(width, -1))
    cross_out_w = gather_out(cross_out_weight)
    expand_w = gather_in(expand_weight.reshape(width, -1))
    contract_w = gather_out(contract_weight)
    params = lax.all_gather(jnp.concatenate([norm_gain, norm_bias], 0), "col", axis=1, tiled=True)
    gains = params[:3].astype(jnp.float32)
    offsets = params[3:].astype(jnp.float32)

    feats = rows_in.astype(jnp.float32)
    head_width = triple_weight.shape[2]
    triple = in_proj(rows_in, triple_w).astype(jnp.bfloat16)
    q1, k1, v1 = (
        to_heads(triple[:, i * head_width : (i + 1) * head_width]) for i in range(3)
    )
    attended_heads, self_lse = self_attend(q1, k1, v1, self_info, own)
    attended = from_heads(attended_heads)
    h1, n1, r1 = norm_forward(
        feats + both_halves(out_proj(attended, self_out_w)), gains[0], offsets[0]
    )
    h1b = h1.astype(jnp.bfloat16)
    q2 = in_proj(h1b, query_w).astype(jnp.bfloat16)
    pairs = lax.all_gather(
        in_proj(memory, memory_w).astype(jnp.bfloat16), "col", axis=0, tiled=True
    )
    crossed, cross_lse = cross_attend(q2, pairs, cross_info, passage_count, PLEN)
    h2, n2, r2 = norm_forward(
        h1 + both_halves(out_proj(crossed, cross_out_w)), gains[1], offsets[1]
    )
    h2b = h2.astype(jnp.bfloat16)
    hidden = in_proj(h2b, expand_w)
    active, gelu_pull = jax.vjp(gelu_exact, hidden)
    active = active.astype(jnp.bfloat16)
    final, n3, r3 = norm_forward(
        h2 + both_halves(out_proj(active, contract_w)), gains[2], offsets[2]
    )

    e_out = upstream.astype(jnp.float32)
    e3 = norm_back(e_out, n3, r3, gains[2])
    gain_three, bias_three = norm_param_sums(e_out, n3, own)
    b3 = e3.astype(jnp.bfloat16)
    contract_grad = reduce_weight(out_weight_grad(active, b3, cols))
    grad_hidden = gelu_pull(out_proj_back(b3, contract_w))[0].astype(jnp.bfloat16)
    expand_grad = reduce_weight(in_weight_grad(h2b, grad_hidden))
    up_two = e3 + both_halves(in_proj_back(grad_hidden, expand_w))
    e2 = norm_back(up_two, n2, r2, gains[1])
    gain_two, bias_two = norm_param_sums(up_two, n2, own)
    b2 = e2.astype(jnp.bfloat16)
    cross_out_grad = reduce_weight(out_weight_grad(crossed, b2, cols))
    grad_crossed = out_proj_back(b2, cross_out_w).astype(jnp.bfloat16)
    dq2, grad_pairs = cross_attend_back(
        q2, pairs, crossed, grad_crossed, cross_lse, cross_info, passage_count, PLEN
    )
    grad_pairs = lax.psum_scatter(grad_pairs, "col", scatter_dimension=0, tiled=True)
    query_grad = reduce_weight(in_weight_grad(h1b, dq2))
    up_one = e2 + both_halves(in_proj_back(dq2, query_w))
    e1 = norm_back(up_one, n1, r1, gains[0])
    gain_one, bias_one = norm_param_sums(up_one, n1, own)
    b1 = e1.astype(jnp.bfloat16)
    memory_grad = reduce_weight(in_weight_grad(memory, grad_pairs))
    memory_part = in_proj_back(grad_pairs, memory_w)
    memory_rows = memory_own.shape[0]
    grad_memory = memory_part[:memory_rows] + swap_row(
        memory_part[memory_rows:].astype(jnp.bfloat16)
    ).astype(jnp.float32)
    grad_passages = to_features(grad_memory[:PLEN].astype(jnp.bfloat16)).reshape(passages.shape)

    self_out_grad = reduce_weight(out_weight_grad(attended, b1, cols))
    grad_attended = to_heads(out_proj_back(b1, self_out_w).astype(jnp.bfloat16))
    heads_back = self_attend_back(
        q1, k1, v1, attended_heads, grad_attended, self_lse, self_info, own
    )
    grad_triple_all = jnp.concatenate([from_heads(g) for g in heads_back], 1)
    triple_grad = reduce_weight(in_weight_grad(rows_in, grad_triple_all))
    input_part = in_proj_back(grad_triple_all, triple_w)
    grad_own = (
        e1[:own]
        + input_part[:own]
        + swap_row(input_part[own:].astype(jnp.bfloat16)).astype(jnp.float32)
    )

    def give_tokens(value):
        return regroup(to_features(value.astype(jnp.bfloat16)), back_select, back_place, groups)

    output = give_tokens(final[:own])
    grad_tokens = give_tokens(grad_own)
    sums = lax.psum(
        jnp.stack([gain_one, gain_two, gain_three, bias_one, bias_two, bias_three]),
        ("dp", "row", "col"),
    )
    sums = lax.dynamic_slice_in_dim(sums, col_index * width, width, 1)
    return (
        output,
        grad_tokens,
        grad_passages,
        triple_grad.reshape(triple_weight.shape),
        self_out_grad,
        query_grad.reshape(query_weight.shape),
        memory_grad.reshape(memory_weight.shape),
        cross_out_grad,
        expand_grad.reshape(expand_weight.shape),
        contract_grad,
        sums[:3],
        sums[3:],
    )


def solution(mesh):
    in_specs = (
        P(("dp", "row"), "col"),
        P(("dp", "row"), None, "col"),
        P(),
        P(),
        P(),
        P("col", None, "row"),
        P("row", "col"),
        P("col", None, "row"),
        P("col", None, "row"),
        P("row", "col"),
        P("col", None, "row"),
        P("row", "col"),
        P(None, "col"),
        P(None, "col"),
        P(("dp", "row"), "col"),
    )
    out_specs = (
        P(("dp", "row"), "col"),
        P(("dp", "row"), "col"),
        P(("dp", "row"), None, "col"),
        P("col", None, "row"),
        P("row", "col"),
        P("col", None, "row"),
        P("col", None, "row"),
        P("row", "col"),
        P("col", None, "row"),
        P("row", "col"),
        P(None, "col"),
        P(None, "col"),
    )
    return jax.shard_map(
        on_device, mesh=mesh, in_specs=in_specs, out_specs=out_specs, check_vma=False
    )
```

```python
import jax
import jax.numpy as jnp
from jax import lax
from jax.experimental import pallas as pl
from jax.experimental.pallas import tpu as pltpu
from jax.sharding import PartitionSpec as P

HD = 64
PAIR = 2 * HD
PLEN = 300
TOPP = 5
PP_GRP = 8
BLK = 128
SPAN = 304


epsilon = 1e-05
LOW = -1e30
FACTOR = HD ** (-0.5)


def swap_row(value):
    return lax.ppermute(value, "row", [(0, 1), (1, 0)])


def swap_dp(value, bit):
    return lax.ppermute(value, "dp", [(i, i ^ bit) for i in range(lax.axis_size("dp"))])


def shift_col(value, step):
    cols = lax.axis_size("col")
    return lax.ppermute(value, "col", [(i, (i + step) % cols) for i in range(cols)])


QUARTERS = 4
LANES = 128


def own_quarter():
    return lax.axis_index("dp") % QUARTERS


def spread(part):
    half = jnp.stack([part, swap_dp(part, 2)])
    return jnp.concatenate([half, swap_dp(half, 1)], 0)


def natural(parts):
    own = own_quarter()
    parts = [parts[k] for k in (0, 2, 1, 3)]
    for bit in (1, 2):
        flip_it = (own & bit) > 0
        parts = [jnp.where(flip_it, parts[k ^ bit], parts[k]) for k in range(QUARTERS)]
    return parts


def collect(halves):
    near = halves[0] + swap_dp(halves[1], 1)
    total = near[0] + swap_dp(near[1], 2)
    total = lax.psum_scatter(
        total.reshape(-1, total.shape[-1]), "col", scatter_dimension=0, tiled=True
    )
    bit = QUARTERS
    while bit < lax.axis_size("dp"):
        total = total + swap_dp(total, bit)
        bit *= 2
    return [p.astype(jnp.float32) for p in natural(spread(total))]


def to_tokens(rows):
    cols = lax.axis_size("col")
    count, width = rows.shape
    got = lax.all_to_all(rows.reshape(cols, count // cols, width), "col", 0, 0, tiled=True)
    return got.transpose(1, 0, 2).reshape(count // cols, cols * width)


def to_features(rows):
    cols = lax.axis_size("col")
    count, width = rows.shape
    parts = rows.reshape(count, cols, width // cols).transpose(1, 0, 2)
    return lax.all_to_all(parts, "col", 0, 0, tiled=True).reshape(count * cols, width // cols)


def to_heads(rows):
    return to_features(rows)


def from_heads(rows):
    return to_tokens(rows)


def regroup(value, select, placing, groups):
    width = value.shape[-1]
    out = value.reshape(-1, BLK, width)[select]
    moved = lax.all_to_all(out, "dp", split_axis=0, concat_axis=0, tiled=True)
    return moved[placing].reshape(-1, width)


def lane_rows(block):
    return jnp.concatenate(
        [block[:, i : i + LANES] for i in range(0, block.shape[1], LANES)], 0
    )


def in_quarter(weight):
    part = weight.shape[2] // QUARTERS
    cut = lax.dynamic_slice_in_dim(weight, own_quarter() * part, part, 2)
    return lane_rows(cut.reshape(weight.shape[0], -1))


def out_quarter(weight):
    part = weight.shape[0] // QUARTERS
    return lane_rows(lax.dynamic_slice_in_dim(weight, own_quarter() * part, part, 0))


def join_in(parts, count):
    split = parts.reshape(QUARTERS, parts.shape[1], -1, count, LANES)
    return split.transpose(1, 3, 0, 2, 4).reshape(split.shape[1] * count, -1)


def join_out(parts, count):
    split = parts.reshape(QUARTERS, parts.shape[1], -1, count, LANES)
    return split.transpose(1, 0, 3, 2, 4).reshape(split.shape[1], QUARTERS * count, -1)


def in_proj(rows, weight):
    return jnp.einsum("tf,fe->te", rows, weight, preferred_element_type=jnp.float32)


def in_proj_back(grad, weight):
    return jnp.einsum("te,fe->tf", grad, weight, preferred_element_type=jnp.float32)


def out_proj(rows, weight):
    out = jnp.einsum("te,cef->tcf", rows, weight, preferred_element_type=jnp.float32)
    return out.reshape(rows.shape[0], -1)


def out_proj_back(grad, weight):
    parts = grad.reshape(grad.shape[0], weight.shape[0], weight.shape[2])
    return jnp.einsum("tcf,cef->te", parts, weight, preferred_element_type=jnp.float32)


def in_weight_grad(rows, grad):
    part = grad.shape[1] // QUARTERS

    def half(k):
        return jnp.stack(
            [
                jnp.einsum(
                    "tf,te->fe",
                    rows,
                    grad[:, j * part : (j + 1) * part],
                    preferred_element_type=jnp.float32,
                ).astype(jnp.bfloat16)
                for j in (2 * k, 2 * k + 1)
            ]
        )

    return [half(0), half(1)]


def out_weight_grad(rows, grad, cols):
    part = rows.shape[1] // QUARTERS
    split = grad.reshape(grad.shape[0], cols, -1)

    def half(k):
        return jnp.stack(
            [
                jnp.einsum(
                    "te,tcf->cef",
                    rows[:, j * part : (j + 1) * part],
                    split,
                    preferred_element_type=jnp.float32,
                ).astype(jnp.bfloat16)
                for j in (2 * k, 2 * k + 1)
            ]
        )

    return [half(0), half(1)]


def in_restored(parts, shape):
    return jnp.concatenate([p.reshape(shape[0], shape[1], -1) for p in parts], 2)


def both_halves(part):
    own = part.shape[0] // 2
    low = part.astype(jnp.bfloat16)
    upper = part[:own] + swap_row(low[own:]).astype(jnp.float32)
    lower = part[own:] + swap_row(low[:own]).astype(jnp.float32)
    return jnp.concatenate([upper, lower], 0)


def norm_forward(value, gain, offset):
    center = jnp.mean(value, 1, keepdims=True)
    moved = value - center
    scale = lax.rsqrt(jnp.mean(moved * moved, 1, keepdims=True) + epsilon)
    normed = moved * scale
    return (normed * gain + offset, normed, scale)


def norm_back(grad, normed, scale, gain):
    scaled = grad * gain
    total = jnp.mean(scaled, 1, keepdims=True)
    crossed = jnp.mean(scaled * normed, 1, keepdims=True)
    return scale * (scaled - total - normed * crossed)


def norm_param_sums(grad, normed, own):
    return (jnp.sum(grad[:own] * normed[:own], 0), jnp.sum(grad[:own], 0))


def nt(left, right):
    return lax.dot_general(
        left, right, (((1,), (1,)), ((), ())), preferred_element_type=jnp.float32
    )


def nn(left, right):
    return jnp.dot(left, right, preferred_element_type=jnp.float32)


def flip(value):
    return value.astype(jnp.float32).T.astype(jnp.bfloat16)


def stack_heads(value):
    lane = lax.broadcasted_iota(jnp.int32, value.shape, 1) // HD
    wide = value.astype(jnp.float32)
    parts = [jnp.where(lane == h, wide, 0.0) for h in range(2)]
    return jnp.concatenate(parts, 0).astype(jnp.bfloat16)


def fresh_state(count):
    return (
        jnp.full((1, count), LOW, jnp.float32),
        jnp.zeros((1, count), jnp.float32),
        jnp.zeros((HD, count), jnp.float32),
    )


def per_head(flipped, wide):
    count = wide.shape[1] // 2
    return jnp.concatenate(
        [nn(flipped[h * HD : (h + 1) * HD], wide[:, h * count : (h + 1) * count]) for h in range(2)],
        1,
    )


def step_forward(state, scores, v_flipped):
    top, total, out = state
    fresh = jnp.maximum(top, jnp.max(scores, 0, keepdims=True))
    keep = jnp.exp(top - fresh)
    expo = jnp.exp(scores - fresh)
    total = total * keep + jnp.sum(expo, 0, keepdims=True)
    out = out * keep + per_head(v_flipped, expo.astype(jnp.bfloat16))
    return (fresh, total, out)


def rows_of(out):
    count = out.shape[1] // 2
    return jnp.concatenate([out[:, :count], out[:, count:]], 0).T


def finish_forward(state, o_ref, lse_ref):
    top, total, out = state
    o_ref[...] = rows_of(out / total).astype(jnp.bfloat16)
    lse_ref[...] = (top + jnp.log(total)).reshape(lse_ref.shape)


def delta_of(out, up):
    both = (out.astype(jnp.float32) * up.astype(jnp.float32)).T
    return jnp.concatenate(
        [jnp.sum(both[h * HD : (h + 1) * HD], 0, keepdims=True) for h in range(2)], 1
    )


def step_backward(scores, lse, delta, value, up, queries, k_flipped):
    probs = jnp.exp(scores - lse)
    grad_value = nn(probs.astype(jnp.bfloat16), up)
    grad_scores = (probs * (nt(value, up) - delta)).astype(jnp.bfloat16)
    return grad_value, nn(grad_scores, queries), per_head(k_flipped, grad_scores)


def self_spans(i, first, tile):
    start = i * tile
    begin = jnp.where(start >= first, first, 0)
    begin_last = jnp.where(start + tile - 1 >= first, first, 0)
    low = begin // tile
    middle = jnp.minimum((begin_last + tile - 1) // tile, i)
    return low, jnp.maximum(middle, low)


def self_masked(scores, i, j, first, tile):
    count = scores.shape[1]
    key_pos = j * tile + lax.broadcasted_iota(jnp.int32, scores.shape, 0)
    lane = lax.broadcasted_iota(jnp.int32, (1, count), 1)
    query_pos = i * tile + jnp.where(lane >= tile, lane - tile, lane)
    begin = jnp.where(query_pos >= first, first, 0)
    return jnp.where((key_pos <= query_pos) & (key_pos >= begin), scores, LOW)


def self_forward_kernel(tiles, tile, info, q_ref, k_ref, v_ref, o_ref, lse_ref, v_flipped):
    i = pl.program_id(0)
    first = info[tiles]

    @pl.when(i == 0)
    def _():
        for j in range(tiles):
            v_flipped[j] = flip(v_ref[j * tile : (j + 1) * tile, :])

    queries = stack_heads(q_ref[...].astype(jnp.float32) * FACTOR)
    low, middle = self_spans(i, first, tile)

    def visit(masked):
        def body(j, state):
            at = info[j]
            keys = k_ref[pl.ds(pl.multiple_of(at * tile, tile), tile), :]
            scores = nt(keys, queries)
            if masked:
                scores = self_masked(scores, i, j, first, tile)
            return step_forward(state, scores, v_flipped[at])

        return body

    state = fresh_state(2 * tile)
    state = lax.fori_loop(low, middle, visit(True), state)
    state = lax.fori_loop(middle, i, visit(False), state)
    finish_forward(visit(True)(i, state), o_ref, lse_ref)


def self_backward_kernel(
    tiles, tile, info, q_ref, k_ref, v_ref, o_ref, up_ref, lse_ref,
    grad_ref, k_flipped, dk_sum, dv_sum,
):
    i = pl.program_id(0)
    first = info[tiles]

    @pl.when(i == 0)
    def _():
        for j in range(tiles):
            k_flipped[j] = flip(k_ref[j * tile : (j + 1) * tile, :])
        dk_sum[...] = jnp.zeros_like(dk_sum)
        dv_sum[...] = jnp.zeros_like(dv_sum)

    queries = stack_heads(q_ref[...].astype(jnp.float32) * FACTOR)
    up = stack_heads(up_ref[...])
    delta = delta_of(o_ref[...], up_ref[...])
    lse = lse_ref[...].reshape(1, 2 * tile)
    low, middle = self_spans(i, first, tile)

    def visit(masked):
        def body(j, total):
            at = info[j]
            rows = pl.ds(pl.multiple_of(at * tile, tile), tile)
            scores = nt(k_ref[rows, :], queries)
            if masked:
                scores = self_masked(scores, i, j, first, tile)
            gv, gk, gq = step_backward(
                scores, lse, delta, v_ref[rows, :], up, queries, k_flipped[at]
            )
            dv_sum[rows, :] += gv
            dk_sum[rows, :] += gk
            return total + gq

        return body

    total = jnp.zeros((HD, 2 * tile), jnp.float32)
    total = lax.fori_loop(low, middle, visit(True), total)
    total = lax.fori_loop(middle, i, visit(False), total)
    total = visit(True)(i, total)
    own = pl.ds(pl.multiple_of(info[i] * tile, tile), tile)
    grad_ref[own, :PAIR] = (rows_of(total) * FACTOR).astype(jnp.bfloat16)

    @pl.when(i == tiles - 1)
    def _():
        grad_ref[:, PAIR : 2 * PAIR] = dk_sum[...].astype(jnp.bfloat16)
        grad_ref[:, 2 * PAIR :] = dv_sum[...].astype(jnp.bfloat16)


def cost(flops, elements, size):
    return pl.CostEstimate(flops=flops, bytes_accessed=size, transcendentals=elements)


def self_specs(total, tile):
    part = pl.BlockSpec((tile, PAIR), lambda i, info: (info[i], 0))
    whole = [pl.BlockSpec((total, PAIR), lambda i, info, c=c: (0, c)) for c in (1, 2)]
    stat = pl.BlockSpec((1, 1, 2 * tile), lambda i, info: (i, 0, 0))
    return part, whole, stat


def self_attend(qkv, info, tile):
    total = qkv.shape[0]
    tiles = total // tile
    part, whole, stat = self_specs(total, tile)
    elements = total * total
    return pl.pallas_call(
        lambda *refs: self_forward_kernel(tiles, tile, *refs),
        out_shape=(
            jax.ShapeDtypeStruct((total, PAIR), jnp.bfloat16),
            jax.ShapeDtypeStruct((tiles, 1, 2 * tile), jnp.float32),
        ),
        grid_spec=pltpu.PrefetchScalarGridSpec(
            num_scalar_prefetch=1,
            grid=(tiles,),
            in_specs=[part] + whole,
            out_specs=(part, stat),
            scratch_shapes=[pltpu.VMEM((tiles, PAIR, tile), jnp.bfloat16)],
        ),
        cost_estimate=cost(8 * elements * PAIR, elements, 4 * total * PAIR * 2),
        name="self_attend",
    )(info, qkv, qkv, qkv)


def self_attend_back(qkv, out, up, lse, info, tile):
    total = qkv.shape[0]
    tiles = total // tile
    part, whole, stat = self_specs(total, tile)
    elements = total * total
    return pl.pallas_call(
        lambda *refs: self_backward_kernel(tiles, tile, *refs),
        out_shape=jax.ShapeDtypeStruct((total, 3 * PAIR), jnp.bfloat16),
        grid_spec=pltpu.PrefetchScalarGridSpec(
            num_scalar_prefetch=1,
            grid=(tiles,),
            in_specs=[part] + whole + [part, part, stat],
            out_specs=pl.BlockSpec((total, 3 * PAIR), lambda i, info: (0, 0)),
            scratch_shapes=[
                pltpu.VMEM((tiles, PAIR, tile), jnp.bfloat16),
                pltpu.VMEM((total, PAIR), jnp.float32),
                pltpu.VMEM((total, PAIR), jnp.float32),
            ],
        ),
        cost_estimate=cost(20 * elements * PAIR, elements, 8 * total * PAIR * 2),
        name="self_attend_back",
    )(info, qkv, qkv, qkv, out, up, lse)


def cross_scores(keys, queries, bias, valid):
    scores = nt(keys, queries) + bias
    tail = scores.shape[0] - 8
    row = lax.broadcasted_iota(jnp.int32, (8, scores.shape[1]), 0)
    return jnp.concatenate(
        [scores[:tail], jnp.where(row < valid - tail, scores[tail:], LOW)], 0
    )


def cross_bias(info, side, passages, at, count):
    base = side * (passages + 2)
    switch = info[base + passages + 1]
    flags = info[2 * (passages + 2) + at]
    lane = lax.broadcasted_iota(jnp.int32, (1, 2 * count), 1)
    place = jnp.where(lane >= count, lane - count, lane)
    reads = jnp.where(place < switch, flags & 1, flags >> 1)
    return jnp.where(reads > 0, 0.0, LOW)


def cross_forward_kernel(passages, span, valid, info, q_ref, k_ref, v_ref, o_ref, lse_ref, v_flipped):
    side = pl.program_id(1)
    count = q_ref.shape[0]

    @pl.when(side == 0)
    def _():
        for j in range(passages):
            v_flipped[j] = flip(v_ref[j * span : (j + 1) * span, :])

    queries = stack_heads(q_ref[...].astype(jnp.float32) * FACTOR)
    base = side * (passages + 2)

    def body(t, state):
        at = info[base + t]
        keys = k_ref[pl.ds(pl.multiple_of(at * span, 16), span), :]
        scores = cross_scores(keys, queries, cross_bias(info, side, passages, at, count), valid)
        return step_forward(state, scores, v_flipped[at])

    state = lax.fori_loop(0, info[base + passages], body, fresh_state(2 * count))
    finish_forward(state, o_ref, lse_ref)


def cross_backward_kernel(
    passages, span, valid, info, q_ref, k_ref, v_ref, o_ref, up_ref, lse_ref,
    dq_ref, dkv_ref, k_flipped, dk_sum, dv_sum,
):
    side = pl.program_id(1)
    count = q_ref.shape[0]

    @pl.when(side == 0)
    def _():
        for j in range(passages):
            k_flipped[j] = flip(k_ref[j * span : (j + 1) * span, :])
        dk_sum[...] = jnp.zeros_like(dk_sum)
        dv_sum[...] = jnp.zeros_like(dv_sum)

    queries = stack_heads(q_ref[...].astype(jnp.float32) * FACTOR)
    up = stack_heads(up_ref[...])
    delta = delta_of(o_ref[...], up_ref[...])
    lse = lse_ref[...].reshape(1, 2 * count)
    base = side * (passages + 2)

    def body(t, total):
        at = info[base + t]
        rows = pl.ds(pl.multiple_of(at * span, 16), span)
        scores = cross_scores(
            k_ref[rows, :], queries, cross_bias(info, side, passages, at, count), valid
        )
        gv, gk, gq = step_backward(scores, lse, delta, v_ref[rows, :], up, queries, k_flipped[at])
        dv_sum[rows, :] += gv
        dk_sum[rows, :] += gk
        return total + gq

    total = jnp.zeros((HD, 2 * count), jnp.float32)
    total = lax.fori_loop(0, info[base + passages], body, total)
    dq_ref[...] = (rows_of(total) * FACTOR).astype(jnp.bfloat16)

    @pl.when(side == 1)
    def _():
        dkv_ref[:, :PAIR] = dk_sum[...].astype(jnp.bfloat16)
        dkv_ref[:, PAIR:] = dv_sum[...].astype(jnp.bfloat16)


def cross_attend(q, kv, info, passages, valid):
    rows, width = q.shape
    keys = kv.shape[0]
    pairs = width // PAIR
    count = rows // 2
    span = keys // passages
    part = pl.BlockSpec((count, PAIR), lambda p, s, info: (s, p))
    k_spec = pl.BlockSpec((keys, PAIR), lambda p, s, info: (0, 2 * p))
    v_spec = pl.BlockSpec((keys, PAIR), lambda p, s, info: (0, 2 * p + 1))
    stat = pl.BlockSpec((1, 1, 1, 2 * count), lambda p, s, info: (p, s, 0, 0))
    elements = rows * keys * 2 * pairs
    return pl.pallas_call(
        lambda *refs: cross_forward_kernel(passages, span, valid, *refs),
        out_shape=(
            jax.ShapeDtypeStruct((rows, width), jnp.bfloat16),
            jax.ShapeDtypeStruct((pairs, 2, 1, 2 * count), jnp.float32),
        ),
        grid_spec=pltpu.PrefetchScalarGridSpec(
            num_scalar_prefetch=1,
            grid=(pairs, 2),
            in_specs=[part, k_spec, v_spec],
            out_specs=(part, stat),
            scratch_shapes=[pltpu.VMEM((passages, PAIR, span), jnp.bfloat16)],
        ),
        cost_estimate=cost(8 * elements * PAIR, elements, kv.size * 2),
        name="cross_attend",
    )(info, q, kv, kv)


def cross_attend_back(q, kv, out, up, lse, info, passages, valid):
    rows, width = q.shape
    keys = kv.shape[0]
    pairs = width // PAIR
    count = rows // 2
    span = keys // passages
    part = pl.BlockSpec((count, PAIR), lambda p, s, info: (s, p))
    k_spec = pl.BlockSpec((keys, PAIR), lambda p, s, info: (0, 2 * p))
    v_spec = pl.BlockSpec((keys, PAIR), lambda p, s, info: (0, 2 * p + 1))
    whole = pl.BlockSpec((keys, 2 * PAIR), lambda p, s, info: (0, p))
    stat = pl.BlockSpec((1, 1, 1, 2 * count), lambda p, s, info: (p, s, 0, 0))
    elements = rows * keys * 2 * pairs
    return pl.pallas_call(
        lambda *refs: cross_backward_kernel(passages, span, valid, *refs),
        out_shape=(
            jax.ShapeDtypeStruct((rows, width), jnp.bfloat16),
            jax.ShapeDtypeStruct((keys, 2 * width), jnp.bfloat16),
        ),
        grid_spec=pltpu.PrefetchScalarGridSpec(
            num_scalar_prefetch=1,
            grid=(pairs, 2),
            in_specs=[part, k_spec, v_spec, part, part, stat],
            out_specs=(part, whole),
            scratch_shapes=[
                pltpu.VMEM((passages, PAIR, span), jnp.bfloat16),
                pltpu.VMEM((keys, PAIR), jnp.float32),
                pltpu.VMEM((keys, PAIR), jnp.float32),
            ],
        ),
        cost_estimate=cost(20 * elements * PAIR, elements, kv.size * 6),
        name="cross_attend_back",
    )(info, q, kv, kv, out, up, lse)


def gelu_exact(value):
    return jax.nn.gelu(value, approximate=False)


def on_device(
    tokens,
    passages,
    lengths,
    block_order,
    passage_ids,
    triple_weight,
    self_out_weight,
    query_weight,
    memory_weight,
    cross_out_weight,
    expand_weight,
    contract_weight,
    norm_gain,
    norm_bias,
    cotangent,
):
    groups = lax.axis_size("dp")
    row_count = lax.axis_size("row")
    cols = lax.axis_size("col")
    group = lax.axis_index("dp")
    row_index = lax.axis_index("row")
    col_index = lax.axis_index("col")
    own_rows, width = tokens.shape
    features = width * cols
    blocks = own_rows // BLK
    capacity = blocks // (groups // 2)
    span = row_count * blocks
    all_blocks = block_order.shape[0]
    block_ids = jnp.arange(blocks, dtype=jnp.int32)
    slot_ids = jnp.arange(groups * capacity, dtype=jnp.int32)
    inverse = (
        jnp.zeros_like(block_order).at[block_order].set(jnp.arange(all_blocks, dtype=jnp.int32))
    )
    own_blocks = (group * row_count + row_index) * blocks + block_ids
    target = inverse[own_blocks] // span
    earlier = block_ids[None, :] < block_ids[:, None]
    ranking = jnp.sum((target[None, :] == target[:, None]) & earlier, 1)
    matches = (target[None, :] == (slot_ids // capacity)[:, None]) & (
        ranking[None, :] == (slot_ids % capacity)[:, None]
    )
    send_select = jnp.sum(jnp.where(matches, block_ids[None, :], 0), 1)
    back_place = target * capacity + ranking
    wanted = block_order[own_blocks]
    source = wanted // span
    within = wanted % blocks
    rank_in = jnp.sum((source[None, :] == source[:, None]) & (within[None, :] < within[:, None]), 1)
    recv_place = source * capacity + rank_in
    back_matches = recv_place[None, :] == slot_ids[:, None]
    back_select = jnp.sum(jnp.where(back_matches, block_ids[None, :], 0), 1)

    total = own_rows * row_count
    own = own_rows // cols
    first = lax.dynamic_slice_in_dim(lengths, group * 2, 1)[0]
    chosen_ids = lax.dynamic_slice(passage_ids, (group * 2, 0), (2, TOPP)) - group * PP_GRP

    tile_ids = jnp.arange(row_count * cols, dtype=jnp.int32)
    self_info = jnp.concatenate(
        [(tile_ids % cols) * row_count + ((tile_ids // cols) ^ row_index), first[None]]
    )
    pool = passages.shape[0]
    held_passage = ((tile_ids // pool) ^ row_index) * pool + tile_ids % pool
    reads = jnp.any(held_passage[None, None, :] == chosen_ids[:, :, None], 1)
    side = jnp.arange(row_count, dtype=jnp.int32)
    switch = jnp.clip(first - (side ^ row_index) * own_rows - col_index * own, 0, own)
    needed = ((switch > 0)[:, None] & reads[0][None]) | ((switch < own)[:, None] & reads[1][None])
    needed = needed.astype(jnp.int32)
    before = jnp.sum(
        needed[:, None, :] * (tile_ids[None, None, :] < tile_ids[None, :, None]), 2
    )
    slots = needed[:, :, None] * (before[:, :, None] == tile_ids[None, None, :])
    listed = jnp.sum(slots * tile_ids[None, :, None], 1)
    per_side = jnp.concatenate([listed, jnp.sum(needed, 1)[:, None], switch[:, None]], 1)
    flags = reads[0].astype(jnp.int32) + 2 * reads[1].astype(jnp.int32)
    cross_info = jnp.concatenate([per_side.reshape(-1), flags]).astype(jnp.int32)
    passage_count = row_count * pool

    def take_tokens(value):
        mine = to_tokens(regroup(value, send_select, recv_place, groups))
        return jnp.concatenate([mine, swap_row(mine)], 0)

    head_width = triple_weight.shape[2]
    chunk = head_width // QUARTERS
    attention = lax.all_gather(
        jnp.concatenate(
            [in_quarter(triple_weight), in_quarter(memory_weight), in_quarter(query_weight)]
            + [out_quarter(self_out_weight), out_quarter(cross_out_weight)],
            0,
        ),
        "col",
    )
    padded = jnp.pad(passages, ((0, 0), (0, SPAN - PLEN), (0, 0))).reshape(-1, width)
    memory_own = lax.all_gather(padded, "col")
    feed = lax.all_gather(
        jnp.concatenate([in_quarter(expand_weight), out_quarter(contract_weight)], 0), "col"
    )
    triple_rows = 3 * width
    triple_w = join_in(spread(attention[:, :triple_rows]), width)
    rows_in = take_tokens(tokens)
    rest = spread(attention[:, triple_rows:])
    cuts = [0, 2 * width, 3 * width, 3 * width + 2 * chunk, 3 * width + 4 * chunk]
    memory_w, query_w = (
        join_in(rest[:, :, cuts[i] : cuts[i + 1]], width) for i in (0, 1)
    )
    self_out_w, cross_out_w = (
        join_out(rest[:, :, cuts[i] : cuts[i + 1]], chunk) for i in (2, 3)
    )
    feed = spread(feed)
    feed_rows = expand_weight.shape[2] // QUARTERS // LANES * width
    expand_w = join_in(feed[:, :, :feed_rows], width)
    contract_w = join_out(feed[:, :, feed_rows:], contract_weight.shape[0] // QUARTERS)
    memory = jnp.concatenate(
        [m.transpose(1, 0, 2).reshape(-1, features) for m in (memory_own, swap_row(memory_own))], 0
    )

    small = jnp.concatenate([norm_gain, norm_bias], 0)
    gathered = jnp.stack([small] + [shift_col(small, step) for step in range(1, cols)])
    order = (col_index - jnp.arange(cols, dtype=jnp.int32)) % cols
    params = gathered[order].transpose(1, 0, 2).reshape(6, -1).astype(jnp.float32)
    gains, offsets = params[:3], params[3:]

    feats = rows_in.astype(jnp.float32)
    qkv = to_heads(in_proj(rows_in, triple_w).astype(jnp.bfloat16))
    cotangent, qkv = lax.optimization_barrier((cotangent, qkv))
    upstream = take_tokens(cotangent)
    attended_heads, self_lse = self_attend(qkv, self_info, own)
    attended = from_heads(attended_heads)
    h1, n1, r1 = norm_forward(
        feats + both_halves(out_proj(attended, self_out_w)), gains[0], offsets[0]
    )
    h1b = h1.astype(jnp.bfloat16)
    q2 = in_proj(h1b, query_w).astype(jnp.bfloat16)
    pairs = in_proj(memory, memory_w).astype(jnp.bfloat16)
    crossed, cross_lse = cross_attend(q2, pairs, cross_info, passage_count, PLEN)
    h2, n2, r2 = norm_forward(
        h1 + both_halves(out_proj(crossed, cross_out_w)), gains[1], offsets[1]
    )
    h2b = h2.astype(jnp.bfloat16)
    hidden = in_proj(h2b, expand_w)
    active, gelu_pull = jax.vjp(gelu_exact, hidden)
    active = active.astype(jnp.bfloat16)
    final, n3, r3 = norm_forward(
        h2 + both_halves(out_proj(active, contract_w)), gains[2], offsets[2]
    )

    e_out = upstream.astype(jnp.float32)
    e3 = norm_back(e_out, n3, r3, gains[2])
    gain_three, bias_three = norm_param_sums(e_out, n3, own)
    b3 = e3.astype(jnp.bfloat16)
    contract_grad = collect(out_weight_grad(active, b3, cols))
    grad_hidden = gelu_pull(out_proj_back(b3, contract_w))[0].astype(jnp.bfloat16)
    expand_grad = collect(in_weight_grad(h2b, grad_hidden))
    up_two = e3 + both_halves(in_proj_back(grad_hidden, expand_w))
    e2 = norm_back(up_two, n2, r2, gains[1])
    gain_two, bias_two = norm_param_sums(up_two, n2, own)
    b2 = e2.astype(jnp.bfloat16)
    cross_out_grad = collect(out_weight_grad(crossed, b2, cols))
    grad_crossed = out_proj_back(b2, cross_out_w).astype(jnp.bfloat16)
    dq2, grad_pairs = cross_attend_back(
        q2, pairs, crossed, grad_crossed, cross_lse, cross_info, passage_count, PLEN
    )
    query_grad = collect(in_weight_grad(h1b, dq2))
    up_one = e2 + both_halves(in_proj_back(dq2, query_w))
    e1 = norm_back(up_one, n1, r1, gains[0])
    gain_one, bias_one = norm_param_sums(up_one, n1, own)
    b1 = e1.astype(jnp.bfloat16)
    memory_grad = collect(in_weight_grad(memory, grad_pairs))
    memory_part = in_proj_back(grad_pairs, memory_w).astype(jnp.bfloat16)
    held = memory.shape[0] // row_count
    away, b1 = lax.optimization_barrier((memory_part[held:], b1))
    grad_memory = memory_part[:held] + swap_row(away)
    grad_memory = lax.psum_scatter(
        grad_memory.reshape(held, cols, width).transpose(1, 0, 2).reshape(-1, width),
        "col",
        scatter_dimension=0,
        tiled=True,
    )
    grad_passages = grad_memory.reshape(pool, SPAN, width)[:, :PLEN]

    self_out_grad = collect(out_weight_grad(attended, b1, cols))
    grad_attended = to_heads(out_proj_back(b1, self_out_w).astype(jnp.bfloat16))
    grad_triple_all = self_attend_back(
        qkv, attended_heads, grad_attended, self_lse, self_info, own
    )
    grad_triple_all = from_heads(grad_triple_all)
    triple_grad = collect(in_weight_grad(rows_in, grad_triple_all))
    input_part = in_proj_back(grad_triple_all, triple_w)
    grad_own = (
        e1[:own]
        + input_part[:own]
        + swap_row(input_part[own:].astype(jnp.bfloat16)).astype(jnp.float32)
    )

    def give_tokens(value):
        return regroup(to_features(value.astype(jnp.bfloat16)), back_select, back_place, groups)

    output = give_tokens(final[:own])
    grad_tokens = give_tokens(grad_own)
    sums = jnp.stack([gain_one, gain_two, gain_three, bias_one, bias_two, bias_three])
    sums = sums + swap_row(sums)
    sums = sums.reshape(6, cols, width).transpose(1, 0, 2)
    total_sums = sums[col_index]
    for step in range(1, cols):
        total_sums = total_sums + shift_col(sums[(col_index + step) % cols], step)
    bit = 1
    while bit < groups:
        total_sums = total_sums + swap_dp(total_sums, bit)
        bit *= 2
    sums = total_sums
    return (
        output,
        grad_tokens,
        grad_passages,
        in_restored(triple_grad, triple_weight.shape),
        jnp.concatenate(self_out_grad, 0),
        in_restored(query_grad, query_weight.shape),
        in_restored(memory_grad, memory_weight.shape),
        jnp.concatenate(cross_out_grad, 0),
        in_restored(expand_grad, expand_weight.shape),
        jnp.concatenate(contract_grad, 0),
        sums[:3],
        sums[3:],
    )


def solution(mesh):
    in_specs = (
        P(("dp", "row"), "col"),
        P(("dp", "row"), None, "col"),
        P(),
        P(),
        P(),
        P("col", None, "row"),
        P("row", "col"),
        P("col", None, "row"),
        P("col", None, "row"),
        P("row", "col"),
        P("col", None, "row"),
        P("row", "col"),
        P(None, "col"),
        P(None, "col"),
        P(("dp", "row"), "col"),
    )
    out_specs = (
        P(("dp", "row"), "col"),
        P(("dp", "row"), "col"),
        P(("dp", "row"), None, "col"),
        P("col", None, "row"),
        P("row", "col"),
        P("col", None, "row"),
        P("col", None, "row"),
        P("row", "col"),
        P("col", None, "row"),
        P("row", "col"),
        P(None, "col"),
        P(None, "col"),
    )
    return jax.shard_map(
        on_device, mesh=mesh, in_specs=in_specs, out_specs=out_specs, check_vma=False
    )
```

```python
import jax
import jax.numpy as jnp
from jax import lax
from jax.experimental import pallas as pl
from jax.experimental.pallas import tpu as pltpu
from jax.sharding import PartitionSpec as P

HD = 64
PAIR = 2 * HD
PLEN = 300
TOPP = 5
PP_GRP = 8
BLK = 128
SPAN = 304


epsilon = 1e-05
LOW = -1e30
FACTOR = HD ** (-0.5)


def swap_row(value):
    return lax.ppermute(value, "row", [(0, 1), (1, 0)])


def swap_dp(value, bit):
    return lax.ppermute(value, "dp", [(i, i ^ bit) for i in range(lax.axis_size("dp"))])


def shift_col(value, step):
    cols = lax.axis_size("col")
    return lax.ppermute(value, "col", [(i, (i + step) % cols) for i in range(cols)])


QUARTERS = 4


def own_quarter():
    return lax.axis_index("dp") % QUARTERS


def tie(*values):
    return lax.optimization_barrier(values)


def spread(part):
    far = swap_dp(part, 2)
    return [part, far, swap_dp(part, 1), swap_dp(far, 1)]


def natural(parts):
    own = own_quarter()
    parts = [parts[k] for k in (0, 2, 1, 3)]
    for bit in (1, 2):
        flip_it = (own & bit) > 0
        parts = [jnp.where(flip_it, parts[k ^ bit], parts[k]) for k in range(QUARTERS)]
    return parts


def near_stage(halves):
    return halves[0] + swap_dp(halves[1], 1)


def far_stage(near, axis):
    part = near.shape[axis] // 2
    own = lax.slice_in_dim(near, 0, part, axis=axis)
    return own + swap_dp(lax.slice_in_dim(near, part, 2 * part, axis=axis), 2)


def col_stage(total):
    total = lax.psum_scatter(total, "col", scatter_dimension=0, tiled=True)
    bit = QUARTERS
    while bit < lax.axis_size("dp"):
        total = total + swap_dp(total, bit)
        bit *= 2
    return total


def last_stage(total):
    return [p.astype(jnp.float32) for p in natural(spread(total))]


def to_tokens(rows):
    cols = lax.axis_size("col")
    count, width = rows.shape
    got = lax.all_to_all(rows.reshape(cols, count // cols, width), "col", 0, 0, tiled=True)
    return got.transpose(1, 0, 2).reshape(count // cols, cols * width)


def to_features(rows):
    cols = lax.axis_size("col")
    count, width = rows.shape
    parts = rows.reshape(count, cols, width // cols).transpose(1, 0, 2)
    return lax.all_to_all(parts, "col", 0, 0, tiled=True).reshape(count * cols, width // cols)


def to_heads(rows):
    return to_features(rows)


def from_heads(rows):
    return to_tokens(rows)


def regroup(value, select, placing, groups):
    width = value.shape[-1]
    out = value.reshape(-1, BLK, width)[select]
    moved = lax.all_to_all(out, "dp", split_axis=0, concat_axis=0, tiled=True)
    return moved[placing].reshape(-1, width)


def in_quarter(weight):
    part = weight.shape[2] // QUARTERS
    cut = lax.dynamic_slice_in_dim(weight, own_quarter() * part, part, 2)
    return cut.reshape(weight.shape[0], -1)


def out_quarter(weight):
    part = weight.shape[0] // QUARTERS
    return lax.dynamic_slice_in_dim(weight, own_quarter() * part, part, 0)


def in_proj(rows, weight):
    return jnp.einsum("tf,fe->te", rows, weight, preferred_element_type=jnp.float32)


def in_proj_back(grad, weight):
    return jnp.einsum("te,fe->tf", grad, weight, preferred_element_type=jnp.float32)


def by_col(total, cols):
    width = total.shape[1] // cols
    return jnp.concatenate([total[:, c * width : (c + 1) * width] for c in range(cols)], 0)


def in_weight_grad(rows, grad):
    part = grad.shape[1] // 2
    return [
        jnp.einsum(
            "tf,te->fe", rows, grad[:, k * part : (k + 1) * part], preferred_element_type=jnp.float32
        ).astype(jnp.bfloat16)
        for k in range(2)
    ]


def out_weight_grad(rows, grad):
    part = rows.shape[1] // 2
    return [
        jnp.einsum(
            "te,tf->ef", rows[:, k * part : (k + 1) * part], grad, preferred_element_type=jnp.float32
        ).astype(jnp.bfloat16)
        for k in range(2)
    ]


def in_restored(parts, shape):
    return jnp.concatenate([p.reshape(shape[0], shape[1], -1) for p in parts], 2)


def both_halves(part, *beside):
    own = part.shape[0] // 2
    low = part.astype(jnp.bfloat16)
    upper, lower = swap_row(low[own:]), swap_row(low[:own])
    if beside:
        upper, lower, *beside = tie(upper, lower, *beside)
    total = part + jnp.concatenate([upper, lower], 0).astype(jnp.float32)
    return (total, *beside) if beside else total


def norm_forward(value, gain, offset):
    center = jnp.mean(value, 1, keepdims=True)
    moved = value - center
    scale = lax.rsqrt(jnp.mean(moved * moved, 1, keepdims=True) + epsilon)
    normed = moved * scale
    return (normed * gain + offset, normed, scale)


def norm_back(grad, normed, scale, gain):
    scaled = grad * gain
    total = jnp.mean(scaled, 1, keepdims=True)
    crossed = jnp.mean(scaled * normed, 1, keepdims=True)
    return scale * (scaled - total - normed * crossed)


def norm_param_sums(grad, normed, own):
    return (jnp.sum(grad[:own] * normed[:own], 0), jnp.sum(grad[:own], 0))


def nt(left, right):
    return lax.dot_general(
        left, right, (((1,), (1,)), ((), ())), preferred_element_type=jnp.float32
    )


def nn(left, right):
    return jnp.dot(left, right, preferred_element_type=jnp.float32)


def flip(value):
    return value.astype(jnp.float32).T.astype(jnp.bfloat16)


def stack_heads(value):
    lane = lax.broadcasted_iota(jnp.int32, value.shape, 1) // HD
    wide = value.astype(jnp.float32)
    parts = [jnp.where(lane == h, wide, 0.0) for h in range(2)]
    return jnp.concatenate(parts, 0).astype(jnp.bfloat16)


def fresh_state(count):
    return (
        jnp.full((1, count), LOW, jnp.float32),
        jnp.zeros((1, count), jnp.float32),
        jnp.zeros((HD, count), jnp.float32),
    )


def per_head(flipped, wide):
    count = wide.shape[1] // 2
    return jnp.concatenate(
        [nn(flipped[h * HD : (h + 1) * HD], wide[:, h * count : (h + 1) * count]) for h in range(2)],
        1,
    )


def step_forward(state, scores, v_flipped):
    top, total, out = state
    fresh = jnp.maximum(top, jnp.max(scores, 0, keepdims=True))
    keep = jnp.exp(top - fresh)
    expo = jnp.exp(scores - fresh)
    total = total * keep + jnp.sum(expo, 0, keepdims=True)
    out = out * keep + per_head(v_flipped, expo.astype(jnp.bfloat16))
    return (fresh, total, out)


def rows_of(out):
    count = out.shape[1] // 2
    return jnp.concatenate([out[:, :count], out[:, count:]], 0).T


def finish_forward(state, o_ref, lse_ref):
    top, total, out = state
    o_ref[...] = rows_of(out / total).astype(jnp.bfloat16)
    lse_ref[...] = (top + jnp.log(total)).reshape(lse_ref.shape)


def delta_of(out, up):
    both = (out.astype(jnp.float32) * up.astype(jnp.float32)).T
    return jnp.concatenate(
        [jnp.sum(both[h * HD : (h + 1) * HD], 0, keepdims=True) for h in range(2)], 1
    )


def step_backward(scores, lse, delta, value, up, queries, k_flipped):
    probs = jnp.exp(scores - lse)
    grad_value = nn(probs.astype(jnp.bfloat16), up)
    grad_scores = (probs * (nt(value, up) - delta)).astype(jnp.bfloat16)
    return grad_value, nn(grad_scores, queries), per_head(k_flipped, grad_scores)


def self_spans(i, first, tile):
    start = i * tile
    begin = jnp.where(start >= first, first, 0)
    begin_last = jnp.where(start + tile - 1 >= first, first, 0)
    low = begin // tile
    middle = jnp.minimum((begin_last + tile - 1) // tile, i)
    return low, jnp.maximum(middle, low)


def self_masked(scores, i, j, first, tile):
    count = scores.shape[1]
    key_pos = j * tile + lax.broadcasted_iota(jnp.int32, scores.shape, 0)
    lane = lax.broadcasted_iota(jnp.int32, (1, count), 1)
    query_pos = i * tile + jnp.where(lane >= tile, lane - tile, lane)
    begin = jnp.where(query_pos >= first, first, 0)
    return jnp.where((key_pos <= query_pos) & (key_pos >= begin), scores, LOW)


def self_forward_kernel(tiles, tile, info, q_ref, k_ref, v_ref, o_ref, lse_ref, v_flipped):
    i = pl.program_id(0)
    first = info[tiles]

    @pl.when(i == 0)
    def _():
        for j in range(tiles):
            v_flipped[j] = flip(v_ref[j * tile : (j + 1) * tile, :])

    queries = stack_heads(q_ref[...].astype(jnp.float32) * FACTOR)
    low, middle = self_spans(i, first, tile)

    def visit(masked):
        def body(j, state):
            at = info[j]
            keys = k_ref[pl.ds(pl.multiple_of(at * tile, tile), tile), :]
            scores = nt(keys, queries)
            if masked:
                scores = self_masked(scores, i, j, first, tile)
            return step_forward(state, scores, v_flipped[at])

        return body

    state = fresh_state(2 * tile)
    state = lax.fori_loop(low, middle, visit(True), state)
    state = lax.fori_loop(middle, i, visit(False), state)
    finish_forward(visit(True)(i, state), o_ref, lse_ref)


def self_backward_kernel(
    tiles, tile, info, q_ref, k_ref, v_ref, o_ref, up_ref, lse_ref,
    grad_ref, k_flipped, dk_sum, dv_sum,
):
    i = pl.program_id(0)
    first = info[tiles]

    @pl.when(i == 0)
    def _():
        for j in range(tiles):
            k_flipped[j] = flip(k_ref[j * tile : (j + 1) * tile, :])
        dk_sum[...] = jnp.zeros_like(dk_sum)
        dv_sum[...] = jnp.zeros_like(dv_sum)

    queries = stack_heads(q_ref[...].astype(jnp.float32) * FACTOR)
    up = stack_heads(up_ref[...])
    delta = delta_of(o_ref[...], up_ref[...])
    lse = lse_ref[...].reshape(1, 2 * tile)
    low, middle = self_spans(i, first, tile)

    def visit(masked):
        def body(j, total):
            at = info[j]
            rows = pl.ds(pl.multiple_of(at * tile, tile), tile)
            scores = nt(k_ref[rows, :], queries)
            if masked:
                scores = self_masked(scores, i, j, first, tile)
            gv, gk, gq = step_backward(
                scores, lse, delta, v_ref[rows, :], up, queries, k_flipped[at]
            )
            dv_sum[rows, :] += gv
            dk_sum[rows, :] += gk
            return total + gq

        return body

    total = jnp.zeros((HD, 2 * tile), jnp.float32)
    total = lax.fori_loop(low, middle, visit(True), total)
    total = lax.fori_loop(middle, i, visit(False), total)
    total = visit(True)(i, total)
    own = pl.ds(pl.multiple_of(info[i] * tile, tile), tile)
    grad_ref[own, :PAIR] = (rows_of(total) * FACTOR).astype(jnp.bfloat16)

    @pl.when(i == tiles - 1)
    def _():
        grad_ref[:, PAIR : 2 * PAIR] = dk_sum[...].astype(jnp.bfloat16)
        grad_ref[:, 2 * PAIR :] = dv_sum[...].astype(jnp.bfloat16)


def cost(flops, elements, size):
    return pl.CostEstimate(flops=flops, bytes_accessed=size, transcendentals=elements)


def self_specs(total, tile):
    part = pl.BlockSpec((tile, PAIR), lambda i, info: (info[i], 0))
    whole = [pl.BlockSpec((total, PAIR), lambda i, info, c=c: (0, c)) for c in (1, 2)]
    stat = pl.BlockSpec((1, 1, 2 * tile), lambda i, info: (i, 0, 0))
    return part, whole, stat


def self_attend(qkv, info, tile):
    total = qkv.shape[0]
    tiles = total // tile
    part, whole, stat = self_specs(total, tile)
    elements = total * total
    return pl.pallas_call(
        lambda *refs: self_forward_kernel(tiles, tile, *refs),
        out_shape=(
            jax.ShapeDtypeStruct((total, PAIR), jnp.bfloat16),
            jax.ShapeDtypeStruct((tiles, 1, 2 * tile), jnp.float32),
        ),
        grid_spec=pltpu.PrefetchScalarGridSpec(
            num_scalar_prefetch=1,
            grid=(tiles,),
            in_specs=[part] + whole,
            out_specs=(part, stat),
            scratch_shapes=[pltpu.VMEM((tiles, PAIR, tile), jnp.bfloat16)],
        ),
        cost_estimate=cost(8 * elements * PAIR, elements, 4 * total * PAIR * 2),
        name="self_attend",
    )(info, qkv, qkv, qkv)


def self_attend_back(qkv, out, up, lse, info, tile):
    total = qkv.shape[0]
    tiles = total // tile
    part, whole, stat = self_specs(total, tile)
    elements = total * total
    return pl.pallas_call(
        lambda *refs: self_backward_kernel(tiles, tile, *refs),
        out_shape=jax.ShapeDtypeStruct((total, 3 * PAIR), jnp.bfloat16),
        grid_spec=pltpu.PrefetchScalarGridSpec(
            num_scalar_prefetch=1,
            grid=(tiles,),
            in_specs=[part] + whole + [part, part, stat],
            out_specs=pl.BlockSpec((total, 3 * PAIR), lambda i, info: (0, 0)),
            scratch_shapes=[
                pltpu.VMEM((tiles, PAIR, tile), jnp.bfloat16),
                pltpu.VMEM((total, PAIR), jnp.float32),
                pltpu.VMEM((total, PAIR), jnp.float32),
            ],
        ),
        cost_estimate=cost(20 * elements * PAIR, elements, 8 * total * PAIR * 2),
        name="self_attend_back",
    )(info, qkv, qkv, qkv, out, up, lse)


def cross_scores(keys, queries, bias, valid):
    scores = nt(keys, queries) + bias
    tail = scores.shape[0] - 8
    row = lax.broadcasted_iota(jnp.int32, (8, scores.shape[1]), 0)
    return jnp.concatenate(
        [scores[:tail], jnp.where(row < valid - tail, scores[tail:], LOW)], 0
    )


def cross_bias(info, side, passages, at, count):
    base = side * (passages + 2)
    switch = info[base + passages + 1]
    flags = info[2 * (passages + 2) + at]
    lane = lax.broadcasted_iota(jnp.int32, (1, 2 * count), 1)
    place = jnp.where(lane >= count, lane - count, lane)
    reads = jnp.where(place < switch, flags & 1, flags >> 1)
    return jnp.where(reads > 0, 0.0, LOW)


def cross_forward_kernel(passages, span, valid, info, q_ref, k_ref, v_ref, o_ref, lse_ref, v_flipped):
    side = pl.program_id(1)
    count = q_ref.shape[0]

    @pl.when(side == 0)
    def _():
        for j in range(passages):
            v_flipped[j] = flip(v_ref[j * span : (j + 1) * span, :])

    queries = stack_heads(q_ref[...].astype(jnp.float32) * FACTOR)
    base = side * (passages + 2)

    def body(t, state):
        at = info[base + t]
        keys = k_ref[pl.ds(pl.multiple_of(at * span, 16), span), :]
        scores = cross_scores(keys, queries, cross_bias(info, side, passages, at, count), valid)
        return step_forward(state, scores, v_flipped[at])

    state = lax.fori_loop(0, info[base + passages], body, fresh_state(2 * count))
    finish_forward(state, o_ref, lse_ref)


def cross_backward_kernel(
    passages, span, valid, info, q_ref, k_ref, v_ref, o_ref, up_ref, lse_ref,
    dq_ref, dkv_ref, k_flipped, dk_sum, dv_sum,
):
    side = pl.program_id(1)
    count = q_ref.shape[0]

    @pl.when(side == 0)
    def _():
        for j in range(passages):
            k_flipped[j] = flip(k_ref[j * span : (j + 1) * span, :])
        dk_sum[...] = jnp.zeros_like(dk_sum)
        dv_sum[...] = jnp.zeros_like(dv_sum)

    queries = stack_heads(q_ref[...].astype(jnp.float32) * FACTOR)
    up = stack_heads(up_ref[...])
    delta = delta_of(o_ref[...], up_ref[...])
    lse = lse_ref[...].reshape(1, 2 * count)
    base = side * (passages + 2)

    def body(t, total):
        at = info[base + t]
        rows = pl.ds(pl.multiple_of(at * span, 16), span)
        scores = cross_scores(
            k_ref[rows, :], queries, cross_bias(info, side, passages, at, count), valid
        )
        gv, gk, gq = step_backward(scores, lse, delta, v_ref[rows, :], up, queries, k_flipped[at])
        dv_sum[rows, :] += gv
        dk_sum[rows, :] += gk
        return total + gq

    total = jnp.zeros((HD, 2 * count), jnp.float32)
    total = lax.fori_loop(0, info[base + passages], body, total)
    dq_ref[...] = (rows_of(total) * FACTOR).astype(jnp.bfloat16)

    @pl.when(side == 1)
    def _():
        dkv_ref[:, :PAIR] = dk_sum[...].astype(jnp.bfloat16)
        dkv_ref[:, PAIR:] = dv_sum[...].astype(jnp.bfloat16)


def cross_attend(q, kv, info, passages, valid):
    rows, width = q.shape
    keys = kv.shape[0]
    pairs = width // PAIR
    count = rows // 2
    span = keys // passages
    part = pl.BlockSpec((count, PAIR), lambda p, s, info: (s, p))
    k_spec = pl.BlockSpec((keys, PAIR), lambda p, s, info: (0, 2 * p))
    v_spec = pl.BlockSpec((keys, PAIR), lambda p, s, info: (0, 2 * p + 1))
    stat = pl.BlockSpec((1, 1, 1, 2 * count), lambda p, s, info: (p, s, 0, 0))
    elements = rows * keys * 2 * pairs
    return pl.pallas_call(
        lambda *refs: cross_forward_kernel(passages, span, valid, *refs),
        out_shape=(
            jax.ShapeDtypeStruct((rows, width), jnp.bfloat16),
            jax.ShapeDtypeStruct((pairs, 2, 1, 2 * count), jnp.float32),
        ),
        grid_spec=pltpu.PrefetchScalarGridSpec(
            num_scalar_prefetch=1,
            grid=(pairs, 2),
            in_specs=[part, k_spec, v_spec],
            out_specs=(part, stat),
            scratch_shapes=[pltpu.VMEM((passages, PAIR, span), jnp.bfloat16)],
        ),
        cost_estimate=cost(8 * elements * PAIR, elements, kv.size * 2),
        name="cross_attend",
    )(info, q, kv, kv)


def cross_attend_back(q, kv, out, up, lse, info, passages, valid):
    rows, width = q.shape
    keys = kv.shape[0]
    pairs = width // PAIR
    count = rows // 2
    span = keys // passages
    part = pl.BlockSpec((count, PAIR), lambda p, s, info: (s, p))
    k_spec = pl.BlockSpec((keys, PAIR), lambda p, s, info: (0, 2 * p))
    v_spec = pl.BlockSpec((keys, PAIR), lambda p, s, info: (0, 2 * p + 1))
    whole = pl.BlockSpec((keys, 2 * PAIR), lambda p, s, info: (0, p))
    stat = pl.BlockSpec((1, 1, 1, 2 * count), lambda p, s, info: (p, s, 0, 0))
    elements = rows * keys * 2 * pairs
    return pl.pallas_call(
        lambda *refs: cross_backward_kernel(passages, span, valid, *refs),
        out_shape=(
            jax.ShapeDtypeStruct((rows, width), jnp.bfloat16),
            jax.ShapeDtypeStruct((keys, 2 * width), jnp.bfloat16),
        ),
        grid_spec=pltpu.PrefetchScalarGridSpec(
            num_scalar_prefetch=1,
            grid=(pairs, 2),
            in_specs=[part, k_spec, v_spec, part, part, stat],
            out_specs=(part, whole),
            scratch_shapes=[
                pltpu.VMEM((passages, PAIR, span), jnp.bfloat16),
                pltpu.VMEM((keys, PAIR), jnp.float32),
                pltpu.VMEM((keys, PAIR), jnp.float32),
            ],
        ),
        cost_estimate=cost(20 * elements * PAIR, elements, kv.size * 6),
        name="cross_attend_back",
    )(info, q, kv, kv, out, up, lse)


def memory_kernel(parts, own_ref, other_ref, w_ref, out_ref):
    i = pl.program_id(0)

    def write(ref):
        width = ref.shape[2]
        total = nn(ref[0], w_ref[:width, :])
        for c in range(1, ref.shape[0]):
            total = total + nn(ref[c], w_ref[c * width : (c + 1) * width, :])
        out_ref[...] = total.astype(jnp.bfloat16)

    @pl.when(i < parts)
    def _():
        write(own_ref)

    @pl.when(i >= parts)
    def _():
        write(other_ref)


def memory_specs(cols, parts, width):
    return [
        pl.BlockSpec((cols, SPAN, width), lambda i: (0, jnp.minimum(i, parts - 1), 0)),
        pl.BlockSpec((cols, SPAN, width), lambda i: (0, jnp.maximum(i - parts, 0), 0)),
    ]


def memory_project(own, other, weight):
    cols, count, width = own.shape
    parts = count // SPAN
    size = weight.shape[1]
    return pl.pallas_call(
        lambda *refs: memory_kernel(parts, *refs),
        out_shape=jax.ShapeDtypeStruct((2 * count, size), jnp.bfloat16),
        grid=(2 * parts,),
        in_specs=memory_specs(cols, parts, width)
        + [pl.BlockSpec(weight.shape, lambda i: (0, 0))],
        out_specs=pl.BlockSpec((SPAN, size), lambda i: (i, 0)),
        cost_estimate=cost(4 * count * cols * width * size, 0, 8 * count * size),
        name="memory_project",
    )(own, other, weight)


def memory_back_kernel(parts, grad_ref, w_ref, own_ref, other_ref):
    i = pl.program_id(0)

    def write(ref):
        width = ref.shape[2]
        for c in range(ref.shape[0]):
            ref[c] = nt(grad_ref[...], w_ref[c * width : (c + 1) * width, :]).astype(jnp.bfloat16)

    @pl.when(i < parts)
    def _():
        write(own_ref)

    @pl.when(i >= parts)
    def _():
        write(other_ref)


def memory_project_back(grad, weight, cols):
    count = grad.shape[0] // 2
    width = weight.shape[0] // cols
    parts = count // SPAN
    size = weight.shape[1]
    like = jax.ShapeDtypeStruct((cols, count, width), jnp.bfloat16)
    return pl.pallas_call(
        lambda *refs: memory_back_kernel(parts, *refs),
        out_shape=(like, like),
        grid=(2 * parts,),
        in_specs=[
            pl.BlockSpec((SPAN, size), lambda i: (i, 0)),
            pl.BlockSpec(weight.shape, lambda i: (0, 0)),
        ],
        out_specs=tuple(memory_specs(cols, parts, width)),
        cost_estimate=cost(4 * count * cols * width * size, 0, 8 * count * size),
        name="memory_project_back",
    )(grad, weight)


def memory_weight_kernel(parts, own_ref, other_ref, grad_ref, first_ref, second_ref, total):
    i = pl.program_id(0)

    @pl.when(i == 0)
    def _():
        total[...] = jnp.zeros_like(total)

    def add(ref):
        width = ref.shape[2]
        for c in range(ref.shape[0]):
            total[c * width : (c + 1) * width, :] += nn(flip(ref[c]), grad_ref[...])

    @pl.when(i < parts)
    def _():
        add(own_ref)

    @pl.when(i >= parts)
    def _():
        add(other_ref)

    @pl.when(i == 2 * parts - 1)
    def _():
        half = first_ref.shape[1]
        first_ref[...] = total[:, :half].astype(jnp.bfloat16)
        second_ref[...] = total[:, half:].astype(jnp.bfloat16)


def memory_weight_grad(own, other, grad):
    cols, count, width = own.shape
    parts = count // SPAN
    size = grad.shape[1]
    like = jax.ShapeDtypeStruct((cols * width, size // 2), jnp.bfloat16)
    half = pl.BlockSpec(like.shape, lambda i: (0, 0))
    return pl.pallas_call(
        lambda *refs: memory_weight_kernel(parts, *refs),
        out_shape=(like, like),
        grid=(2 * parts,),
        in_specs=memory_specs(cols, parts, width) + [pl.BlockSpec((SPAN, size), lambda i: (i, 0))],
        out_specs=(half, half),
        scratch_shapes=[pltpu.VMEM((cols * width, size), jnp.float32)],
        cost_estimate=cost(4 * count * cols * width * size, 0, 8 * count * size),
        name="memory_weight_grad",
    )(own, other, grad)


def join_kernel(pieces, *refs):
    k = pl.program_id(0)
    out_ref = refs[-1]
    count = out_ref.shape[0]
    width = out_ref.shape[1] // pieces
    for j, ref in enumerate(refs[:-1]):

        @pl.when(k == j)
        def _(ref=ref):
            for c in range(pieces):
                out_ref[:, c * width : (c + 1) * width] = ref[c * count : (c + 1) * count, :]


def join_out(parts, column, width, features):
    rows = parts[0].shape[0]
    pieces = features // width
    count = rows // pieces
    return pl.pallas_call(
        lambda *refs: join_kernel(pieces, *refs),
        out_shape=jax.ShapeDtypeStruct((QUARTERS * count, features), jnp.bfloat16),
        grid=(QUARTERS,),
        in_specs=[pl.BlockSpec((rows, width), lambda k: (0, column))] * QUARTERS,
        out_specs=pl.BlockSpec((count, features), lambda k: (k, 0)),
        cost_estimate=cost(0, 0, 4 * QUARTERS * count * features),
        name="join_out",
    )(*parts)


def gelu_exact(value):
    return jax.nn.gelu(value, approximate=False)


def on_device(
    tokens,
    passages,
    lengths,
    block_order,
    passage_ids,
    triple_weight,
    self_out_weight,
    query_weight,
    memory_weight,
    cross_out_weight,
    expand_weight,
    contract_weight,
    norm_gain,
    norm_bias,
    cotangent,
):
    groups = lax.axis_size("dp")
    row_count = lax.axis_size("row")
    cols = lax.axis_size("col")
    group = lax.axis_index("dp")
    row_index = lax.axis_index("row")
    col_index = lax.axis_index("col")
    own_rows, width = tokens.shape
    features = width * cols
    blocks = own_rows // BLK
    capacity = blocks // (groups // 2)
    span = row_count * blocks
    all_blocks = block_order.shape[0]
    block_ids = jnp.arange(blocks, dtype=jnp.int32)
    slot_ids = jnp.arange(groups * capacity, dtype=jnp.int32)
    inverse = (
        jnp.zeros_like(block_order).at[block_order].set(jnp.arange(all_blocks, dtype=jnp.int32))
    )
    own_blocks = (group * row_count + row_index) * blocks + block_ids
    target = inverse[own_blocks] // span
    earlier = block_ids[None, :] < block_ids[:, None]
    ranking = jnp.sum((target[None, :] == target[:, None]) & earlier, 1)
    matches = (target[None, :] == (slot_ids // capacity)[:, None]) & (
        ranking[None, :] == (slot_ids % capacity)[:, None]
    )
    send_select = jnp.sum(jnp.where(matches, block_ids[None, :], 0), 1)
    back_place = target * capacity + ranking
    wanted = block_order[own_blocks]
    source = wanted // span
    within = wanted % blocks
    rank_in = jnp.sum((source[None, :] == source[:, None]) & (within[None, :] < within[:, None]), 1)
    recv_place = source * capacity + rank_in
    back_matches = recv_place[None, :] == slot_ids[:, None]
    back_select = jnp.sum(jnp.where(back_matches, block_ids[None, :], 0), 1)

    total = own_rows * row_count
    own = own_rows // cols
    first = lax.dynamic_slice_in_dim(lengths, group * 2, 1)[0]
    chosen_ids = lax.dynamic_slice(passage_ids, (group * 2, 0), (2, TOPP)) - group * PP_GRP

    tile_ids = jnp.arange(row_count * cols, dtype=jnp.int32)
    self_info = jnp.concatenate(
        [(tile_ids % cols) * row_count + ((tile_ids // cols) ^ row_index), first[None]]
    )
    pool = passages.shape[0]
    held_passage = ((tile_ids // pool) ^ row_index) * pool + tile_ids % pool
    reads = jnp.any(held_passage[None, None, :] == chosen_ids[:, :, None], 1)
    side = jnp.arange(row_count, dtype=jnp.int32)
    switch = jnp.clip(first - (side ^ row_index) * own_rows - col_index * own, 0, own)
    needed = ((switch > 0)[:, None] & reads[0][None]) | ((switch < own)[:, None] & reads[1][None])
    needed = needed.astype(jnp.int32)
    before = jnp.sum(
        needed[:, None, :] * (tile_ids[None, None, :] < tile_ids[None, :, None]), 2
    )
    slots = needed[:, :, None] * (before[:, :, None] == tile_ids[None, None, :])
    listed = jnp.sum(slots * tile_ids[None, :, None], 1)
    per_side = jnp.concatenate([listed, jnp.sum(needed, 1)[:, None], switch[:, None]], 1)
    flags = reads[0].astype(jnp.int32) + 2 * reads[1].astype(jnp.int32)
    cross_info = jnp.concatenate([per_side.reshape(-1), flags]).astype(jnp.int32)
    passage_count = row_count * pool

    chunk = triple_weight.shape[2] // QUARTERS

    def as_columns(block):
        return jnp.concatenate([block[:, :chunk], block[:, chunk:]], 0)

    inner = lax.all_gather(
        jnp.concatenate(
            [in_quarter(triple_weight), in_quarter(memory_weight), in_quarter(query_weight)]
            + [as_columns(out_quarter(w)) for w in (self_out_weight, cross_out_weight)],
            1,
        ),
        "col",
        axis=0,
        tiled=True,
    )
    mine = to_tokens(regroup(tokens, send_select, recv_place, groups))
    padded = jnp.pad(passages, ((0, 0), (0, SPAN - PLEN), (0, 0))).reshape(-1, width)
    mine, inner, padded = tie(mine, inner, padded)
    memory_own = lax.all_gather(padded, "col")
    triple_w = jnp.concatenate(spread(inner[:, : 3 * chunk]), 1)
    rest = spread(inner[:, 3 * chunk :])
    rows_in = jnp.concatenate([mine, swap_row(mine)], 0)

    small = jnp.concatenate([norm_gain, norm_bias], 0)
    gathered = jnp.stack([small] + [shift_col(small, step) for step in range(1, cols)])
    order = (col_index - jnp.arange(cols, dtype=jnp.int32)) % cols
    params = gathered[order].transpose(1, 0, 2).reshape(6, -1).astype(jnp.float32)
    gains, offsets = params[:3], params[3:]

    feats = rows_in.astype(jnp.float32)
    qkv, memory_own = tie(in_proj(rows_in, triple_w).astype(jnp.bfloat16), memory_own)
    near_part, far_part = swap_row(memory_own[: cols // 2]), swap_row(memory_own[cols // 2 :])
    qkv, near_part, contract_part, expand_part = tie(
        to_heads(qkv), near_part, out_quarter(contract_weight), in_quarter(expand_weight)
    )
    memory_w = jnp.concatenate([p[:, : 2 * chunk] for p in rest], 1)
    query_w = jnp.concatenate([p[:, 2 * chunk : 3 * chunk] for p in rest], 1)
    self_out_w = join_out(rest, 3, chunk, features)
    cross_out_w = join_out(rest, 4, chunk, features)
    expand_w = jnp.concatenate(
        spread(lax.all_gather(expand_part, "col", axis=0, tiled=True)), 1
    )
    contract_w = join_out(
        spread(lax.all_gather(contract_part, "col", axis=0, tiled=True)), 0, width, features
    )
    attended_heads, self_lse = self_attend(qkv, self_info, own)
    attended, far_part = tie(from_heads(attended_heads), far_part)
    memory_other = jnp.concatenate([near_part, far_part], 0)
    branch, pairs = both_halves(
        in_proj(attended, self_out_w), memory_project(memory_own, memory_other, memory_w)
    )
    h1, n1, r1 = norm_forward(feats + branch, gains[0], offsets[0])
    h1b, cotangent = tie(h1.astype(jnp.bfloat16), cotangent)
    up_moved = regroup(cotangent, send_select, recv_place, groups)
    q2 = in_proj(h1b, query_w).astype(jnp.bfloat16)
    crossed, cross_lse = cross_attend(q2, pairs, cross_info, passage_count, PLEN)
    crossed, up_moved = tie(crossed, up_moved)
    h2, n2, r2 = norm_forward(
        h1 + both_halves(in_proj(crossed, cross_out_w)), gains[1], offsets[1]
    )
    h2b, up_mine = tie(h2.astype(jnp.bfloat16), to_tokens(up_moved))
    up_other = swap_row(up_mine)
    hidden = in_proj(h2b, expand_w)
    active, gelu_pull = jax.vjp(gelu_exact, hidden)
    active, up_other = tie(active.astype(jnp.bfloat16), up_other)
    upstream = jnp.concatenate([up_mine, up_other], 0)
    final, n3, r3 = norm_forward(
        h2 + both_halves(in_proj(active, contract_w)), gains[2], offsets[2]
    )

    e_out = upstream.astype(jnp.float32)
    e3 = norm_back(e_out, n3, r3, gains[2])
    gain_three, bias_three = norm_param_sums(e_out, n3, own)
    b3 = e3.astype(jnp.bfloat16)
    contract_near = near_stage(out_weight_grad(active, b3))
    grad_hidden = gelu_pull(in_proj_back(b3, contract_w))[0].astype(jnp.bfloat16)
    expand_near = near_stage(in_weight_grad(h2b, grad_hidden))
    up_two = e3 + both_halves(in_proj_back(grad_hidden, expand_w))
    e2 = norm_back(up_two, n2, r2, gains[1])
    gain_two, bias_two = norm_param_sums(up_two, n2, own)
    b2, contract_near, expand_near, final = tie(
        e2.astype(jnp.bfloat16), contract_near, expand_near, final[:own].astype(jnp.bfloat16)
    )
    contract_total = far_stage(contract_near, 0)
    cross_out_near = near_stage(out_weight_grad(crossed, b2))
    grad_crossed = in_proj_back(b2, cross_out_w).astype(jnp.bfloat16)
    dq2, grad_pairs = cross_attend_back(
        q2, pairs, crossed, grad_crossed, cross_lse, cross_info, passage_count, PLEN
    )
    dq2, grad_pairs, contract_total, expand_near, final = tie(
        dq2, grad_pairs, contract_total, expand_near, to_features(final)
    )
    output = regroup(final, back_select, back_place, groups)
    contract_grad = col_stage(by_col(contract_total, cols))
    expand_total = far_stage(expand_near, 1)
    query_near = near_stage(in_weight_grad(h1b, dq2))
    branch, kept, away = both_halves(
        in_proj_back(dq2, query_w), *memory_project_back(grad_pairs, memory_w, cols)
    )
    up_one = e2 + branch
    e1 = norm_back(up_one, n1, r1, gains[0])
    gain_one, bias_one = norm_param_sums(up_one, n1, own)
    b1, away, expand_total, cross_out_near, query_near, output, grad_pairs = tie(
        e1.astype(jnp.bfloat16), away, expand_total, cross_out_near, query_near, output, grad_pairs
    )
    expand_grad = col_stage(expand_total)
    grad_attended = to_heads(in_proj_back(b1, self_out_w).astype(jnp.bfloat16))
    grad_memory = kept + swap_row(away)
    memory_near = near_stage(memory_weight_grad(memory_own, memory_other, grad_pairs))
    self_out_near = near_stage(out_weight_grad(attended, b1))
    sums = jnp.stack([gain_one, gain_two, gain_three, bias_one, bias_two, bias_three])
    outer_total = by_col(
        jnp.concatenate([far_stage(self_out_near, 0), far_stage(cross_out_near, 0)], 0), cols
    )
    grad_attended, contract_grad, expand_grad, memory_near = tie(
        grad_attended, contract_grad, expand_grad, memory_near
    )
    inner_total = jnp.concatenate([far_stage(memory_near, 1), far_stage(query_near, 1)], 1)
    grad_triple_all = self_attend_back(
        qkv, attended_heads, grad_attended, self_lse, self_info, own
    )
    grad_triple_all, grad_memory = tie(grad_triple_all, grad_memory)
    grad_memory = lax.psum_scatter(
        grad_memory.reshape(-1, width), "col", scatter_dimension=0, tiled=True
    )
    grad_triple_all = from_heads(grad_triple_all)
    grad_triple_all, inner_total, outer_total = tie(grad_triple_all, inner_total, outer_total)
    outer_grad = col_stage(outer_total)
    inner_grad = col_stage(inner_total)
    input_part = in_proj_back(grad_triple_all, triple_w)
    away, halves, contract_grad, expand_grad, sums = tie(
        input_part[own:].astype(jnp.bfloat16),
        in_weight_grad(rows_in, grad_triple_all),
        contract_grad,
        expand_grad,
        sums,
    )
    triple_near = near_stage(halves)
    grad_own = e1[:own] + input_part[:own] + swap_row(away).astype(jnp.float32)
    grad_own, grad_memory = tie(to_features(grad_own.astype(jnp.bfloat16)), grad_memory)
    grad_tokens = regroup(grad_own, back_select, back_place, groups)
    triple_grad = last_stage(col_stage(far_stage(triple_near, 1)))
    inner_grad = last_stage(inner_grad)
    outer_grad = last_stage(outer_grad)
    expand_grad = last_stage(expand_grad)
    contract_grad = last_stage(contract_grad)
    grad_passages = grad_memory.reshape(pool, SPAN, width)[:, :PLEN]
    sums = sums + swap_row(sums)
    memory_grad = [p[:, : 2 * chunk] for p in inner_grad]
    query_grad = [p[:, 2 * chunk :] for p in inner_grad]
    self_out_grad = [p[:chunk] for p in outer_grad]
    cross_out_grad = [p[chunk:] for p in outer_grad]
    sums = sums.reshape(6, cols, width).transpose(1, 0, 2)
    total_sums = sums[col_index]
    for step in range(1, cols):
        total_sums = total_sums + shift_col(sums[(col_index + step) % cols], step)
    bit = 1
    while bit < groups:
        total_sums = total_sums + swap_dp(total_sums, bit)
        bit *= 2
    sums = total_sums
    return (
        output,
        grad_tokens,
        grad_passages,
        in_restored(triple_grad, triple_weight.shape),
        jnp.concatenate(self_out_grad, 0),
        in_restored(query_grad, query_weight.shape),
        in_restored(memory_grad, memory_weight.shape),
        jnp.concatenate(cross_out_grad, 0),
        in_restored(expand_grad, expand_weight.shape),
        jnp.concatenate(contract_grad, 0),
        sums[:3],
        sums[3:],
    )


def solution(mesh):
    in_specs = (
        P(("dp", "row"), "col"),
        P(("dp", "row"), None, "col"),
        P(),
        P(),
        P(),
        P("col", None, "row"),
        P("row", "col"),
        P("col", None, "row"),
        P("col", None, "row"),
        P("row", "col"),
        P("col", None, "row"),
        P("row", "col"),
        P(None, "col"),
        P(None, "col"),
        P(("dp", "row"), "col"),
    )
    out_specs = (
        P(("dp", "row"), "col"),
        P(("dp", "row"), "col"),
        P(("dp", "row"), None, "col"),
        P("col", None, "row"),
        P("row", "col"),
        P("col", None, "row"),
        P("col", None, "row"),
        P("row", "col"),
        P("col", None, "row"),
        P("row", "col"),
        P(None, "col"),
        P(None, "col"),
    )
    return jax.shard_map(
        on_device, mesh=mesh, in_specs=in_specs, out_specs=out_specs, check_vma=False
    )
```
